512 devices in a mesh: table: 64 (over y, z), dp: 8 (over x, core).
Axes of the slice: x: 4, y: 4, z: 16, core: 2. Of those that a mesh axis runs over, the one named last changes fastest.
Arguments:
- emb_table: float32 [131072, 128], P('table'), may hold values from -4 to 4
- versions: int32 [131072], P('table'), may hold values from 0 to 999
- conf_local: int32 [16384], P('table'), may hold values from 0 to 2047, as said below
- conf_version: int32 [16384], P('table'), may hold values from 0 to 999
- conf_values: float32 [16384, 128], P('table'), may hold values from -4 to 4
- owners: int32 [65536, 26, 1], P(('table', 'dp')), may hold values from 0 to 63; in each aligned block of 3328 rows (0 to 3327, 3328 to 6655, ..., all dimensions but the last counted through in order) at most 78 rows name the same one
- row_local: int32 [65536, 26, 2], P(('table', 'dp')), may hold values from 0 to 2047
- lengths: int32 [65536, 26], P(('table', 'dp')), may hold values from 1 to 2
- dense_out: bfloat16 [65536, 128], P(('table', 'dp')), may hold values from -6 to 6
- labels: int32 [65536], P(('table', 'dp')), may hold values 0 or 1
- cross_down: bfloat16 [1, 3456, 512], P(None, None, 'dp'), may hold values from -0.109375 to 0.109375
- cross_up: bfloat16 [1, 512, 3456], P(None, 'dp'), may hold values from -0.25 to 0.25
- cross_bias: float32 [1, 3456], replicated, may hold values from -3 to 3
- head_weight: float32 [3456], replicated, may hold values from -0.109375 to 0.109375
Outputs:
- logits: float32 [65536], P(('table', 'dp'))
- emb_grad: float32 [131072, 128], P(('table', 'dp'))
The draws below stay inside these ranges and needn't reach their ends.
Inputs may be any that keep to these rules, and one draw needn't show every extreme that they name: `owners`: in each aligned block of the 3328 bags of one device (samples in order, bags within a sample in order), at most 78 bags name one holder; in some block one holder is named by exactly 78 bags. `conf_local`: within each holder's 256 entries the local row numbers are distinct.
All inputs are finite; a program needn't handle non-finite values. No bound on the sum of `labels` on one device may be relied on, other than what follows from the above.
Results may differ from the reference program's by a relative error of at most 0.0035.
Values may be sent and summed in bfloat16 or wider, within the bound.
A program may use at most 64 MiB of HBM per device.

```python
import math
import jax
import jax.numpy as jnp
import numpy as np
from jax import lax

E = 128
F = 26
RANK = 512
LAYERS = 1
L = 2
B_DEV = 128
ROWS_DEV = 2048
CONF = 256
XW = 3456
CAP = 78
B = 65536
ROWS = 131072
NCONF = 16384
N_TABLE = 64


def draw_conf_local(key, part):
    holders = NCONF // CONF
    keys = jax.random.split(jax.random.fold_in(key, 11), holders)
    picks = jax.vmap(lambda single: jax.random.permutation(single, ROWS_DEV)[:CONF])(keys)
    parity = jnp.arange(holders, dtype=jnp.int32) % 2
    wanted = jnp.where(parity == 0, ROWS_DEV - 1, 0).astype(jnp.int32)
    offset = (wanted - picks[:, 0].astype(jnp.int32)) % ROWS_DEV
    shifted = (picks.astype(jnp.int32) + offset[:, None]) % ROWS_DEV
    return shifted.reshape(NCONF).astype(jnp.int32)


def place_ends(array, rng, low, high):
    longest = array.shape.index(max(array.shape))
    spots = []
    for shift in (0, 1):
        where = [jax.random.randint(jax.random.fold_in(rng, axis), (), 0, length) for axis, length in enumerate(array.shape)]
        where[longest] = (where[longest] + shift) % array.shape[longest]
        spots.append(tuple(where))
    return array.at[spots[0]].set(low).at[spots[1]].set(high)


def block_scale(own_key, shape, cuts, least, largest):
    gain = 1.0
    for axis_at, blocks in cuts:
        draws = jax.random.uniform(jax.random.fold_in(jax.random.fold_in(own_key, 6), axis_at), (blocks,), jnp.float32, least / len(cuts), largest / len(cuts))
        gain = gain * jnp.repeat(jnp.exp(draws), shape[axis_at] // blocks).reshape((-1,) + (1,) * (len(shape) - 1 - axis_at))
    return gain


def cumulative_ranks(count, skew):
    portions = [(1 << 20) // math.isqrt(grade ** skew) + 1 for grade in range(1, count + 1)]
    deviation = 1 + sum(portions) // (1 << 30)
    return np.cumsum(np.array([max(1, weight // deviation) for weight in portions]))


def ranked_ids(own_key, dims, number_of, skew):
    grid = cumulative_ranks(number_of, skew)
    pick = jax.random.randint(jax.random.fold_in(own_key, 1), dims, 0, int(grid[number_of - 1]))
    standing = jnp.searchsorted(jnp.asarray(grid, jnp.int32), pick, side="right")
    return jax.random.permutation(jax.random.fold_in(own_key, 2), number_of)[standing].astype(jnp.int32)


def assign_block(stream_key, own, number, rows, number_of, top, bound, skew):
    order = jax.random.permutation(stream_key, number_of)
    heavy_load, common = portions_of(number_of, rows * top, bound, skew, True), portions_of(number_of, rows * top, bound, skew, False)
    places = jnp.arange(number_of)

    def named(sizes, turn):
        used = int((sizes > 0).sum())
        fixed = max(1, used // 4)
        moved = fixed + (places - fixed + turn * (used - fixed)) % max(1, number_of - fixed)
        return jnp.zeros((number_of,), jnp.int32).at[order[jnp.where(places < fixed, places, moved)]].set(jnp.asarray(sizes, jnp.int32))

    sizes = jnp.where(number % 4 == 0, named(heavy_load, number // 4), named(common, number - number // 4 - 1))
    mixed = jax.random.permutation(jax.random.fold_in(own, 3), number_of)
    giver, taker = mixed[0:number_of // 2 * 2:2], mixed[1:number_of // 2 * 2:2]
    room = jnp.minimum(sizes[giver] - 1, bound - sizes[taker]) // 2
    room = jnp.where((giver == order[0]) | (taker == order[0]) | (sizes[taker] == 0), 0, jnp.maximum(room, 0))
    moved = jax.random.randint(jax.random.fold_in(own, 4), (number_of // 2,), 0, 1 << 20) % (room + 1)
    sizes = sizes.at[giver].add(-moved).at[taker].add(moved)
    members = jnp.searchsorted(jnp.cumsum(sizes), jnp.arange(rows * top), side="right").astype(jnp.int32)
    listing = members.reshape(top, rows).T
    listing = listing[jax.random.permutation(jax.random.fold_in(own, 1), rows)]
    turn = jax.random.randint(jax.random.fold_in(own, 2), (rows, 1), 0, top)
    return jnp.take_along_axis(listing, (jnp.arange(top)[None, :] + turn) % top, axis=1)


def portions_of(number_of, total, reach, slope, full):
    loads = [(1 << 20) // math.isqrt(rank ** slope) + 1 for rank in range(1, number_of + 1)]
    largest = reach if full else min(reach, max(-(-total // number_of), total * loads[0] // sum(loads)))
    least = 1 if total - largest >= number_of - 1 else 0
    holding, spare = [largest] + [least] * (number_of - 1), total - largest - least * (number_of - 1)
    while spare > 0:
        movable = [i for i in range(1, number_of) if holding[i] < largest] or [i for i in range(1, number_of) if holding[i] < reach]
        mass, left = sum([loads[i] for i in movable]), spare
        for i in movable:
            extra = min(reach - holding[i], max(1, left * loads[i] // mass), spare)
            holding[i] = holding[i] + extra
            spare = spare - extra
    return np.array(holding)


def scatter_about(own_key, dims, scale, bound, cuts=(), kind=jnp.bfloat16):
    drawn = jax.random.normal(own_key, dims, jnp.float32) * scale
    if len(cuts) > 0:
        drawn = block_scale(own_key, dims, cuts, -0.22, 0.18) * drawn
    return jnp.clip(drawn, min=-bound, max=bound).astype(kind)


def setup_inputs(seed: int = 0) -> dict:
    seeds = jax.random.split(jax.random.key(seed), 15)
    emb_table = scatter_about(seeds[0], (ROWS, E), 0.5, 4.0, ((0, 64),), jnp.float32)
    versions = place_ends(jax.random.randint(seeds[1], (ROWS,), 0, 1000), jax.random.fold_in(seeds[1], 1), 0, 999).astype(jnp.int32)
    conf_local = draw_conf_local(jax.random.fold_in(seeds[14], 71), 0)
    conf_version = place_ends(jax.random.randint(seeds[3], (NCONF,), 0, 1000), jax.random.fold_in(seeds[3], 1), 0, 999).astype(jnp.int32)
    conf_values = scatter_about(seeds[4], (NCONF, E), 0.5, 4.0, ((0, 64),), jnp.float32)
    owners_keys = jax.random.split(jax.random.fold_in(seeds[5], 1), B * F // (B_DEV * F))
    owners_turns = jax.random.permutation(jax.random.fold_in(seeds[5], 3), B * F // (B_DEV * F))
    owners = jax.vmap(lambda own, number: assign_block(jax.random.fold_in(seeds[5], 2), own, number, B_DEV * F, N_TABLE, 1, CAP, 2))(owners_keys, owners_turns).reshape((B, F, 1))
    row_local = place_ends(ranked_ids(seeds[6], (B, F, L), ROWS_DEV, 2), jax.random.fold_in(seeds[6], 3), 0, ROWS_DEV - 1).astype(jnp.int32)
    lengths = place_ends(jax.random.randint(seeds[7], (B, F), 1, L + 1), jax.random.fold_in(seeds[7], 1), 1, L).astype(jnp.int32)
    dense_out = scatter_about(seeds[8], (B, E), 1.0, 6.0, ((0, 512),))
    labels = place_ends((jax.random.randint(seeds[9], (B,), 0, 4) < 1).astype(jnp.int32), jax.random.fold_in(seeds[9], 1), 0, 1)
    cross_down = scatter_about(seeds[10], (LAYERS, XW, RANK), XW ** -0.5, 0.109375, ((2, 8),))
    cross_up = scatter_about(seeds[11], (LAYERS, RANK, XW), RANK ** -0.5, 0.25, ((1, 8),))
    cross_bias = scatter_about(seeds[12], (LAYERS, XW), 0.5, 3.0, (), jnp.float32)
    head_weight = scatter_about(seeds[13], (XW,), XW ** -0.5, 0.109375, (), jnp.float32)
    return dict(emb_table=emb_table, versions=versions, conf_local=conf_local, conf_version=conf_version, conf_values=conf_values, owners=owners, row_local=row_local, lengths=lengths, dense_out=dense_out, labels=labels, cross_down=cross_down, cross_up=cross_up, cross_bias=cross_bias, head_weight=head_weight)


loss_scale = 64.0


def dense_step(inputs, labels, cross_down, cross_up, cross_bias, head_weight):
    base_float = inputs.astype(jnp.float32)
    state = base_float
    state_in = inputs
    factors = []
    layer_count = cross_down.shape[0]
    for cross_index in range(layer_count):
        crossed = jnp.dot(state_in, cross_down[cross_index], preferred_element_type=jnp.float32).astype(jnp.bfloat16)
        factor = jnp.dot(crossed, cross_up[cross_index], preferred_element_type=jnp.float32) + cross_bias[cross_index]
        factors.append(factor)
        state = base_float * factor + state
        state_in = state.astype(jnp.bfloat16)
    logits = jnp.sum(state * head_weight, axis=1)
    signal = loss_scale * (jax.nn.sigmoid(logits) - labels.astype(jnp.float32))
    grad_state = signal[:, None] * head_weight[None, :]
    grad_base = jnp.zeros_like(grad_state)
    for cross_index in range(layer_count - 1, -1, -1):
        grad_base = grad_base + grad_state * factors[cross_index]
        grad_lift = (grad_state * base_float).astype(jnp.bfloat16)
        grad_cross = lax.dot_general(grad_lift, cross_up[cross_index], (((1,), (1,)), ((), ())), preferred_element_type=jnp.float32).astype(jnp.bfloat16)
        grad_state = grad_state + lax.dot_general(grad_cross, cross_down[cross_index], (((1,), (1,)), ((), ())), preferred_element_type=jnp.float32)
    return logits, grad_state + grad_base


def reference(emb_table, versions, conf_local, conf_version, conf_values, owners, row_local, lengths, dense_out, labels, cross_down, cross_up, cross_bias, head_weight):
    holder = (jnp.arange(NCONF) // CONF).astype(jnp.int32)
    target = holder * ROWS_DEV + conf_local.astype(jnp.int32)
    is_newer = conf_version > versions[target]
    updated = emb_table.at[target].set(jnp.where(is_newer[:, None], conf_values, emb_table[target]))
    row_ids = (owners * ROWS_DEV + row_local).astype(jnp.int32)
    live_mask = jnp.arange(L, dtype=jnp.int32)[None, None, :] < lengths[:, :, None]
    per_block = B // N_TABLE
    block_ids = row_ids.reshape(N_TABLE, per_block, F, L)
    block_live = live_mask.reshape(N_TABLE, per_block, F, L)
    block_dense = dense_out.reshape(N_TABLE, per_block, E)
    block_labels = labels.reshape(N_TABLE, per_block)

    def scan_step(accumulated, pieces):
        piece_ids, piece_live, piece_dense, piece_labels = pieces
        looked_up = jnp.where(piece_live[..., None], updated[piece_ids], 0.0)
        pooled = jnp.sum(looked_up, axis=2).reshape(per_block, F * E)
        inputs = jnp.concatenate([piece_dense.astype(jnp.float32), pooled], axis=1).astype(jnp.bfloat16)
        piece_logits, grad_input = dense_step(inputs, piece_labels, cross_down, cross_up, cross_bias, head_weight)
        bag_grad = grad_input[:, E:].reshape(per_block, F, 1, E)
        updates = jnp.where(piece_live[..., None], bag_grad, 0.0)
        accumulated = accumulated.at[piece_ids.reshape(-1)].add(updates.reshape(-1, E))
        return accumulated, piece_logits

    start_grad = jnp.zeros((ROWS, E), jnp.float32)
    emb_grad, logit_blocks = lax.scan(scan_step, start_grad, (block_ids, block_live, block_dense, block_labels))
    return logit_blocks.reshape(B), emb_grad
```

```python
import functools
import jax
import jax.numpy as jnp
from jax import lax
from jax.experimental import pallas as pl
from jax.experimental.pallas import tpu as pltpu
from jax.sharding import PartitionSpec as P

loss_scale = 64.0
SLOTS = 80
LANES = 128
VM = pltpu.VMEM
NT = (((1,), (1,)), ((), ()))


def vspec():
    return pl.BlockSpec(memory_space=pltpu.VMEM)


def request_kernel(own_ref, row_ref, len_ref, req_ref, pos_ref, acc_ref):
    features, samples = own_ref.shape
    peers = req_ref.shape[0]
    dead = jnp.int32(2048)
    up = lax.broadcasted_iota(jnp.int32, (samples, samples), 0) < lax.broadcasted_iota(
        jnp.int32, (samples, samples), 1
    )
    before = jnp.where(up, 1.0, 0.0).astype(jnp.bfloat16)
    ones = jnp.ones((samples, samples), jnp.bfloat16)
    holder = lax.broadcasted_iota(jnp.int32, (peers, samples), 0)
    slot = lax.broadcasted_iota(jnp.int32, (SLOTS, samples), 0).astype(jnp.float32)
    acc_ref[...] = jnp.zeros_like(acc_ref)

    def step(f, carry):
        own = own_ref[pl.ds(f, 1), :]
        hit = own == holder
        onehot = jnp.where(hit, 1.0, 0.0)
        narrow = onehot.astype(jnp.bfloat16)
        prior = jnp.dot(narrow, before, preferred_element_type=jnp.float32) + carry
        rank = jnp.sum(onehot * prior, axis=0, keepdims=True)
        carry = carry + jnp.dot(narrow, ones, preferred_element_type=jnp.float32)
        pos_ref[pl.ds(f, 1), :] = own * SLOTS + rank.astype(jnp.int32)
        rows = row_ref[f]
        first = rows[0:1, :]
        second = jnp.where(len_ref[pl.ds(f, 1), :] > 1, rows[1:2, :], dead)
        at = slot == rank
        pieces = []
        for value in (first, second):
            for part in (value // 128, value % 128):
                pieces.append(jnp.where(at, part.astype(jnp.float32), 0.0))
        placed = jnp.concatenate(pieces, axis=0).astype(jnp.bfloat16)
        mark = jnp.where(at, 1.0, 0.0).astype(jnp.bfloat16)
        placed = jnp.concatenate([placed, mark], axis=0)
        acc_ref[...] += lax.dot_general(narrow, placed, NT, preferred_element_type=jnp.float32)
        return carry

    lax.fori_loop(0, features, step, jnp.zeros((peers, samples), jnp.float32))
    acc = acc_ref[...]
    filled = acc[:, 4 * SLOTS : 5 * SLOTS] > 0.5
    for q in range(2):
        high = acc[:, 2 * q * SLOTS : (2 * q + 1) * SLOTS]
        low = acc[:, (2 * q + 1) * SLOTS : (2 * q + 2) * SLOTS]
        ids = jnp.where(filled, (high * 128.0 + low).astype(jnp.int32), dead)
        req_ref[:, q, :] = ids


def build_requests(own, rows, lens, peers):
    features, samples = own.shape
    return pl.pallas_call(
        request_kernel,
        out_shape=(
            jax.ShapeDtypeStruct((peers, 2, SLOTS), jnp.int32),
            jax.ShapeDtypeStruct((features, samples), jnp.int32),
        ),
        in_specs=[vspec()] * 3,
        out_specs=(vspec(), vspec()),
        scratch_shapes=[VM((peers, 5 * SLOTS), jnp.float32)],
        name="requests",
    )(own, rows, lens)


def update_kernel(ver_ref, loc_ref, cver_ref, table_ref, conf_ref, out_ref, work_ref):
    work_ref[...] = table_ref[...]

    def step(block, carry):
        for u in range(8):
            i = block * 8 + u
            g = loc_ref[i]

            @pl.when(cver_ref[i] > ver_ref[g])
            def _():
                work_ref[pl.ds(g, 1), :] = conf_ref[pl.ds(i, 1), :]

        return carry

    lax.fori_loop(0, conf_ref.shape[0] // 8, step, 0)
    now = work_ref[...]
    high = now.astype(jnp.bfloat16)
    out_ref[:, 0:LANES] = high
    out_ref[:, LANES : 2 * LANES] = (now - high.astype(jnp.float32)).astype(jnp.bfloat16)


def update_table(versions, conf_local, conf_version, table, conf_values):
    smem = pl.BlockSpec(memory_space=pltpu.SMEM)
    return pl.pallas_call(
        update_kernel,
        out_shape=jax.ShapeDtypeStruct((table.shape[0], 2 * LANES), jnp.bfloat16),
        in_specs=[smem, smem, smem, vspec(), vspec()],
        out_specs=vspec(),
        scratch_shapes=[VM(table.shape, jnp.float32)],
        name="update",
    )(versions, conf_local, conf_version, table, conf_values)


GROUP = 8


def lookup_kernel(req_ref, table_ref, out_ref, hot_ref):
    blocks = table_ref.shape[0] // LANES
    lane = lax.broadcasted_iota(jnp.int32, (SLOTS, LANES), 1)
    zero = jnp.zeros((SLOTS, LANES), jnp.bfloat16)
    columns = [jnp.transpose(req_ref[:, q, :]) for q in range(2)]
    for u in range(GROUP):
        low, high = [], []
        for q in range(2):
            ids = jnp.broadcast_to(columns[q][:, u : u + 1], (SLOTS, LANES))
            low.append(jnp.where((ids & 127) == lane, 1.0, 0.0).astype(jnp.bfloat16))
            high.append((ids >> 7).astype(jnp.float32).astype(jnp.bfloat16))
        for k in range(blocks):
            k16 = jnp.bfloat16(k)
            hot = jnp.where(high[0] == k16, low[0], zero) + jnp.where(high[1] == k16, low[1], zero)
            hot_ref[u * SLOTS : (u + 1) * SLOTS, k * LANES : (k + 1) * LANES] = hot
    both = jnp.dot(hot_ref[...], table_ref[...], preferred_element_type=jnp.float32)
    out_ref[...] = (both[:, :LANES] + both[:, LANES:]).astype(jnp.bfloat16)


def lookup(req, table):
    peers = req.shape[0]
    rows = table.shape[0]
    return pl.pallas_call(
        lookup_kernel,
        out_shape=jax.ShapeDtypeStruct((peers * SLOTS, LANES), jnp.bfloat16),
        grid=(peers // GROUP,),
        in_specs=[
            pl.BlockSpec((GROUP, 2, SLOTS), lambda g: (g, 0, 0)),
            pl.BlockSpec((rows, 2 * LANES), lambda g: (0, 0)),
        ],
        out_specs=pl.BlockSpec((GROUP * SLOTS, LANES), lambda g: (g, 0)),
        scratch_shapes=[VM((GROUP * SLOTS, rows), jnp.bfloat16)],
        name="lookup",
    )(req, table)


def scatter_kernel(ids_ref, grad_ref, out_ref, hot_ref):
    rows = out_ref.shape[0]
    blocks = rows // LANES
    line = lax.broadcasted_iota(jnp.int32, (LANES, LANES), 0)
    zero = jnp.zeros((LANES, LANES), jnp.bfloat16)
    per = GROUP * SLOTS // LANES

    @pl.when(pl.program_id(0) == 0)
    def _():
        out_ref[...] = jnp.zeros_like(out_ref)

    for c in range(per):
        low, high = [], []
        for q in range(2):
            ids = ids_ref[0, q, c : c + 1, :]
            low.append(jnp.where((ids & 127) == line, 1.0, 0.0).astype(jnp.bfloat16))
            wide = jnp.broadcast_to((ids >> 7).astype(jnp.float32), (LANES, LANES))
            high.append(wide.astype(jnp.bfloat16))
        for k in range(blocks):
            k16 = jnp.bfloat16(k)
            hot = jnp.where(high[0] == k16, low[0], zero) + jnp.where(high[1] == k16, low[1], zero)
            hot_ref[k * LANES : (k + 1) * LANES, c * LANES : (c + 1) * LANES] = hot
    out_ref[...] += jnp.dot(hot_ref[...], grad_ref[...], preferred_element_type=jnp.float32)


def scatter_add(ids, grad, rows):
    groups, _, per, _ = ids.shape
    return pl.pallas_call(
        scatter_kernel,
        out_shape=jax.ShapeDtypeStruct((rows, LANES), jnp.float32),
        grid=(groups,),
        in_specs=[
            pl.BlockSpec((1, 2, per, LANES), lambda g: (g, 0, 0, 0)),
            pl.BlockSpec((GROUP * SLOTS, LANES), lambda g: (g, 0)),
        ],
        out_specs=pl.BlockSpec((rows, LANES), lambda g: (0, 0)),
        scratch_shapes=[VM((rows, GROUP * SLOTS), jnp.bfloat16)],
        name="scatter",
    )(ids, grad)


def middle_kernel(
    pos_ref, ans_ref, dense_ref, label_ref, bias_ref, head_ref, down_hbm, up_hbm,
    logit_ref, send_ref,
    rows_ref, base_ref, factor_ref, back_ref, down_ref, up_ref, sems,
):
    samples = dense_ref.shape[0]
    features = pos_ref.shape[0]
    width = base_ref.shape[2]
    loads = [
        pltpu.make_async_copy(down_hbm, down_ref, sems.at[0]),
        pltpu.make_async_copy(up_hbm, up_ref, sems.at[1]),
    ]
    for load in loads:
        load.start()
    rows_ref[...] = ans_ref[...].astype(jnp.float32)
    base_ref[:, :, 0:LANES] = dense_ref[...].astype(jnp.float32).reshape(samples // 8, 8, LANES)

    def fetch(block, carry):
        b0 = block * 8
        for f in range(features):
            for u in range(8):
                row = rows_ref[pl.ds(pos_ref[f, b0 + u], 1), :]
                base_ref[block, u : u + 1, (f + 1) * LANES : (f + 2) * LANES] = row
        return carry

    lax.fori_loop(0, samples // 8, fetch, 0)
    inputs = base_ref[...].reshape(samples, width).astype(jnp.bfloat16)
    loads[0].wait()
    crossed = lax.dot_general(inputs, down_ref[...], NT, preferred_element_type=jnp.float32)
    crossed = crossed.astype(jnp.bfloat16)
    loads[1].wait()
    base = inputs.astype(jnp.float32)
    head = head_ref[...]
    factor = jnp.dot(crossed, up_ref[...], preferred_element_type=jnp.float32) + bias_ref[...]
    factor_ref[...] = factor
    logits = jnp.sum((base * factor + base) * head, axis=1, keepdims=True)
    logit_ref[...] = logits
    signal = loss_scale * (jax.nn.sigmoid(logits) - label_ref[...].astype(jnp.float32))
    lift = (signal * head * base).astype(jnp.bfloat16)
    cross = lax.dot_general(lift, up_ref[...], NT, preferred_element_type=jnp.float32)
    cross = cross.astype(jnp.bfloat16)
    state = signal * head
    back = (
        state
        + jnp.dot(cross, down_ref[...], preferred_element_type=jnp.float32)
        + state * factor_ref[...]
    )
    back_ref[...] = back.reshape(samples // 8, 8, width)
    rows_ref[...] = jnp.zeros_like(rows_ref)

    def place(block, carry):
        b0 = block * 8
        for f in range(features):
            for u in range(8):
                row = back_ref[block, u : u + 1, (f + 1) * LANES : (f + 2) * LANES]
                rows_ref[pl.ds(pos_ref[f, b0 + u], 1), :] = row
        return carry

    lax.fori_loop(0, samples // 8, place, 0)
    send_ref[...] = rows_ref[...].astype(jnp.bfloat16)


def middle(pos, answer, dense_out, labels, bias, head, down, up):
    samples = dense_out.shape[0]
    rank, width = down.shape
    total = answer.shape[0]
    smem = pl.BlockSpec(memory_space=pltpu.SMEM)
    hbm = pl.BlockSpec(memory_space=pl.ANY)
    return pl.pallas_call(
        middle_kernel,
        out_shape=(
            jax.ShapeDtypeStruct((samples, 1), jnp.float32),
            jax.ShapeDtypeStruct((total, LANES), jnp.bfloat16),
        ),
        in_specs=[smem, vspec(), vspec(), vspec(), vspec(), vspec(), hbm, hbm],
        out_specs=(vspec(), vspec()),
        scratch_shapes=[
            VM((total, LANES), jnp.float32),
            VM((samples // 8, 8, width), jnp.float32),
            VM((samples, width), jnp.float32),
            VM((samples // 8, 8, width), jnp.float32),
            VM((rank, width), jnp.bfloat16),
            VM((rank, width), jnp.bfloat16),
            pltpu.SemaphoreType.DMA((2,)),
        ],
        compiler_params=pltpu.CompilerParams(vmem_limit_bytes=40 << 20),
        name="middle",
    )(pos, answer, dense_out, labels, bias, head, down, up)


def body(
    emb_table, versions, conf_local, conf_version, conf_values, owners, row_local, lengths,
    dense_out, labels, cross_down, cross_up, cross_bias, head_weight,
):
    peers = lax.axis_size("table")
    copies = lax.axis_size("dp")
    rows_dev, emb_width = emb_table.shape
    samples, features, slot_count = row_local.shape
    own = owners.reshape(samples, features).T
    rows = jnp.transpose(row_local, (1, 2, 0))
    req, pos = build_requests(own, rows, lengths.T, peers)
    down_local = cross_down[0].T
    down = lax.all_gather(down_local, "dp", axis=0, tiled=True)
    up = lax.all_gather(cross_up[0], "dp", axis=0, tiled=True)
    asked = lax.all_to_all(req, "table", split_axis=0, concat_axis=0, tiled=True)
    table = update_table(versions, conf_local, conf_version, emb_table, conf_values)
    found = lookup(asked, table).reshape(peers, SLOTS, emb_width)
    answer = lax.all_to_all(found, "table", split_axis=0, concat_axis=0, tiled=True)
    flat = asked.reshape(peers // GROUP, GROUP, 2, SLOTS).transpose(0, 2, 1, 3)
    flat = flat.reshape(peers // GROUP, 2, GROUP * SLOTS // LANES, LANES)
    logits, send = middle(
        pos,
        answer.reshape(peers * SLOTS, emb_width),
        dense_out,
        labels.reshape(samples, 1),
        cross_bias,
        head_weight.reshape(1, -1),
        down,
        up,
    )
    got = lax.all_to_all(
        send.reshape(peers, SLOTS, emb_width), "table", split_axis=0, concat_axis=0, tiled=True
    )
    local = scatter_add(flat, got.reshape(peers * SLOTS, emb_width), rows_dev)
    emb_grad = lax.psum_scatter(local, "dp", scatter_dimension=0, tiled=True)
    return (logits.reshape(samples), emb_grad)


def solution(mesh):
    in_specs = (
        P("table", None),
        P("table"),
        P("table"),
        P("table"),
        P("table", None),
        P(("table", "dp"), None, None),
        P(("table", "dp"), None, None),
        P(("table", "dp"), None),
        P(("table", "dp"), None),
        P(("table", "dp")),
        P(None, None, "dp"),
        P(None, "dp", None),
        P(),
        P(),
    )
    out_specs = (P(("table", "dp")), P(("table", "dp"), None))
    return jax.shard_map(body, mesh=mesh, in_specs=in_specs, out_specs=out_specs, check_vma=False)
```

```python
import jax
import jax.numpy as jnp
from jax import lax
from jax.experimental import pallas as pl
from jax.experimental.pallas import tpu as pltpu
from jax.sharding import PartitionSpec as P

loss_scale = 64.0
PEERS = 64
COPIES = 8
RING_Y = 4
RING_Z = 16
SLOTS = 80
LANES = 128
GROUP = 8
DEAD = 2048
PARTS = 7
VM = pltpu.VMEM
MESH = pl.DeviceIdType.MESH
NT = (((1,), (1,)), ((), ()))
BF = jnp.bfloat16
F32 = jnp.float32


def offset_of(j):
    t = j % RING_Z
    half = (t + 1) // 2
    odd = t % 2
    return j // RING_Z, odd * half + (1 - odd) * (RING_Z - half)


def shifted(j, here, sign):
    dy, dz = offset_of(j)
    y = (here // RING_Z + RING_Y + sign * dy) % RING_Y
    z = (here % RING_Z + 2 * RING_Z + sign * dz) % RING_Z
    return y * RING_Z + z


def slot_of_owner(own, here):
    dy = (own // RING_Z - here // RING_Z + RING_Y) & (RING_Y - 1)
    dz = (own % RING_Z - here % RING_Z + RING_Z) & (RING_Z - 1)
    t = jnp.where(dz == 0, 0, jnp.where(dz <= RING_Z // 2, 2 * dz - 1, 2 * (RING_Z - dz)))
    return dy * RING_Z + t


def step_kernel(
    own_ref, row_ref, len_ref, ver_ref, loc_ref, cver_ref, table_ref, conf_ref,
    dense_ref, label_ref, downl_ref, upl_ref, bias_ref, head_ref,
    logit_ref, out_ref,
    hits_ref, prior_ref, wide_ref, placed_ref, req_ref, asked_ref, pos_v, inv_v, pos_s, inv_s,
    tab_ref, hot_ref, found_ref, ans_ref, rows_ref, base_ref, factor_ref, back_ref,
    down_ref, up_ref, stage_ref, gsend_ref, grecv_ref, hot2_ref, acc_ref, rsend_ref, rrecv_ref,
    q_send, q_recv, a_send, a_recv, g_send, g_recv, w_send, w_recv, c_send, c_recv, r_send, r_recv,
    l_sem,
):
    table_at = lax.axis_index("table")
    dp_at = lax.axis_index("dp")
    features, samples = own_ref.shape
    total = PEERS * SLOTS
    width = bias_ref.shape[1]
    shard = downl_ref.shape[0]
    blocks = table_ref.shape[0] // LANES

    barrier = pltpu.get_barrier_semaphore()

    def greet(j, carry):
        pl.semaphore_signal(
            barrier, inc=1, device_id=(shifted(j, table_at, 1), dp_at), device_id_type=MESH
        )
        return carry

    lax.fori_loop(1, PEERS, greet, 0)
    for k in range(1, COPIES):
        pl.semaphore_signal(
            barrier, inc=1, device_id=(table_at, (dp_at + k) % COPIES), device_id_type=MESH
        )

    grecv_ref[:, SLOTS:LANES, :] = jnp.zeros((PEERS, LANES - SLOTS, LANES), BF)
    acc_ref[...] = jnp.zeros_like(acc_ref)

    holder = lax.broadcasted_iota(jnp.int32, (PEERS, samples), 0)

    def mark_hits(f, carry):
        hit = jnp.where(slot_of_owner(own_ref[pl.ds(f, 1), :], table_at) == holder, 1.0, 0.0)
        hit = hit.astype(BF)
        hits_ref[pl.ds(pl.multiple_of(f * PEERS, PEERS), PEERS), :] = hit
        wide_ref[:, pl.ds(pl.multiple_of(f * LANES, LANES), LANES)] = hit
        return carry

    lax.fori_loop(0, features, mark_hits, 0)
    row_at = lax.broadcasted_iota(jnp.int32, (samples, 2 * samples), 0)
    col_at = lax.broadcasted_iota(jnp.int32, (samples, 2 * samples), 1)
    before = jnp.where((row_at < col_at) | (col_at >= samples), 1.0, 0.0).astype(BF)
    prior_ref[...] = jnp.dot(hits_ref[...], before, preferred_element_type=F32)
    slot = lax.broadcasted_iota(jnp.int32, (SLOTS, samples), 0).astype(F32)
    sample = lax.broadcasted_iota(jnp.int32, (1, samples), 1).astype(F32)

    def rank_bags(f, carry):
        at = pl.ds(pl.multiple_of(f * PEERS, PEERS), PEERS)
        onehot = hits_ref[at, :].astype(F32)
        rank = jnp.sum(onehot * (prior_ref[at, 0:samples] + carry), axis=0, keepdims=True)
        owner = slot_of_owner(own_ref[pl.ds(f, 1), :], table_at)
        pos_v[pl.ds(f, 1), :] = owner * SLOTS + jnp.clip(rank.astype(jnp.int32), 0, SLOTS - 1)
        both = row_ref[f]
        first = both[0:1, :]
        second = jnp.where(len_ref[pl.ds(f, 1), :] > 1, both[1:2, :], DEAD)
        here = slot == rank
        lanes = pl.ds(pl.multiple_of(f * LANES, LANES), LANES)
        values = []
        for value in (first, second):
            values.append((value >> 7).astype(F32))
            values.append((value & 127).astype(F32))
        values.append(jnp.broadcast_to(f.astype(F32), (1, samples)))
        values.append(sample)
        values.append(jnp.ones((1, samples), F32))
        for p, value in enumerate(values):
            placed = jnp.where(here, value, 0.0).astype(BF)
            placed_ref[p * SLOTS : (p + 1) * SLOTS, lanes] = placed
        return carry + prior_ref[at, samples : 2 * samples]

    lax.fori_loop(0, features, rank_bags, jnp.zeros((PEERS, samples), F32))
    packed = lax.dot_general(wide_ref[...], placed_ref[...], NT, preferred_element_type=F32)
    part = [packed[:, p * SLOTS : (p + 1) * SLOTS] for p in range(PARTS)]
    filled = part[6] > 0.5
    dead_tail = jnp.full((PEERS, LANES - SLOTS), DEAD, jnp.int32)
    for q in range(2):
        ids = (part[2 * q] * 128.0 + part[2 * q + 1]).astype(jnp.int32)
        ids = jnp.where(filled, ids, DEAD)
        req_ref[:, q, :] = jnp.concatenate([ids, dead_tail], axis=1)
    inverse = (part[4] * 128.0 + part[5]).astype(jnp.int32)
    inverse = jnp.clip(inverse, 0, features * samples - 1)
    inv_v[...] = jnp.concatenate([inverse, jnp.zeros_like(dead_tail)], axis=1)

    to_smem = [
        pltpu.make_async_copy(pos_v, pos_s, l_sem.at[0]),
        pltpu.make_async_copy(inv_v, inv_s, l_sem.at[1]),
    ]
    for copy in to_smem:
        copy.start()
    own_request = pltpu.make_async_copy(req_ref.at[0], asked_ref.at[0], l_sem.at[2])
    own_request.start()

    pl.semaphore_wait(barrier, PEERS - 1 + COPIES - 1)

    def request_copy(j):
        return pltpu.make_async_remote_copy(
            src_ref=req_ref.at[j], dst_ref=asked_ref.at[j],
            send_sem=q_send.at[j], recv_sem=q_recv.at[j],
            device_id=(shifted(j, table_at, 1), dp_at), device_id_type=MESH,
        )

    def send_request(j, carry):
        request_copy(j).start()
        return carry

    lax.fori_loop(1, PEERS, send_request, 0)

    core, chip = dp_at % 2, dp_at // 2
    chips = COPIES // 2
    weights = ((downl_ref, down_ref), (upl_ref, up_ref))

    def shard_rows(d):
        return pl.ds(pl.multiple_of(d * shard, shard), shard)

    def across(w, k):
        local, full = weights[w]
        return pltpu.make_async_remote_copy(
            src_ref=local, dst_ref=full.at[shard_rows(dp_at)],
            send_sem=w_send.at[w, k], recv_sem=w_recv.at[w, k],
            device_id=(table_at, ((chip + k) % chips) * 2 + core), device_id_type=MESH,
        )

    def pass_on(w, k):
        local, full = weights[w]
        rows = shard_rows(((chip - k + chips) % chips) * 2 + core)
        return pltpu.make_async_remote_copy(
            src_ref=local if k == 0 else full.at[rows], dst_ref=full.at[rows],
            send_sem=c_send.at[w, k], recv_sem=c_recv.at[w, k],
            device_id=(table_at, chip * 2 + 1 - core), device_id_type=MESH,
        )

    own_weights = []
    for w in range(2):
        for k in (1, 3, 2):
            across(w, k).start()
        pass_on(w, 0).start()
        copy = pltpu.make_async_copy(
            weights[w][0], weights[w][1].at[shard_rows(dp_at)], l_sem.at[3 + w]
        )
        copy.start()
        own_weights.append(copy)

    confs = conf_ref.shape[0]
    versions = ver_ref[...]
    pair = jnp.concatenate(
        [(versions >> 7).astype(F32), (versions & 127).astype(F32)]
        + [jnp.zeros((6, versions.shape[1]), F32)], axis=0,
    ).astype(BF)
    local = loc_ref[...]
    line = lax.broadcasted_iota(jnp.int32, (LANES, confs), 0)

    def seen(k, carry):
        hit = jnp.where(line + k * LANES == local, 1.0, 0.0).astype(BF)
        hot2_ref[pl.ds(pl.multiple_of(k * LANES, LANES), LANES), 0:confs] = hit
        return carry

    lax.fori_loop(0, blocks, seen, 0)
    current = jnp.dot(pair, hot2_ref[:, 0:confs], preferred_element_type=F32)
    current = current[0:1, :] * 128.0 + current[1:2, :]
    newer = jnp.where(cver_ref[...].astype(F32) > current, 1.0, 0.0)
    conf = conf_ref[...]
    conf_high = conf.astype(BF)
    conf_low = (conf - conf_high.astype(F32)).astype(BF)
    fresh = jnp.concatenate([conf_high, conf_low, jnp.ones((confs, LANES), BF)], axis=1)

    def renew(k, carry):
        at = pl.ds(pl.multiple_of(k * LANES, LANES), LANES)
        mask = (hot2_ref[at, 0:confs].astype(F32) * newer).astype(BF)
        got = jnp.dot(mask, fresh, preferred_element_type=F32)
        now = table_ref[at, :]
        high = now.astype(BF).astype(F32)
        take = got[:, 2 * LANES : 3 * LANES] > 0.5
        tab_ref[at, 0:LANES] = jnp.where(take, got[:, 0:LANES], high).astype(BF)
        low = jnp.where(take, got[:, LANES : 2 * LANES], now - high)
        tab_ref[at, LANES : 2 * LANES] = low.astype(BF)
        return carry

    lax.fori_loop(0, blocks, renew, 0)

    own_request.wait()
    lane = lax.broadcasted_iota(jnp.int32, (SLOTS, LANES), 1)
    zero = jnp.zeros((SLOTS, LANES), BF)

    def chunk(ref, j):
        return ref.at[pl.ds(pl.multiple_of(j * SLOTS, SLOTS), SLOTS)]

    def answer_copy(j):
        return pltpu.make_async_remote_copy(
            src_ref=chunk(found_ref, j), dst_ref=chunk(ans_ref, j),
            send_sem=a_send.at[j], recv_sem=a_recv.at[j],
            device_id=(shifted(j, table_at, -1), dp_at), device_id_type=MESH,
        )

    own_answer = pltpu.make_async_copy(
        found_ref.at[0:SLOTS], ans_ref.at[0:SLOTS], l_sem.at[5]
    )

    def send_answers(g):
        for u in range(GROUP):
            j = g * GROUP + u
            if u == 0:

                @pl.when(j > 0)
                def _():
                    answer_copy(j).start()

            else:
                answer_copy(j).start()

    def answer_group(g, carry):
        lines = []
        for u in range(GROUP):
            j = g * GROUP + u
            if u == 0:

                @pl.when(j > 0)
                def _():
                    request_copy(j).wait_recv()

            else:
                request_copy(j).wait_recv()
            lines.append(asked_ref[j])
        columns = jnp.transpose(jnp.concatenate(lines, axis=0))
        for u in range(GROUP):
            low, high = [], []
            for q in range(2):
                at = 2 * u + q
                ids = jnp.broadcast_to(columns[0:SLOTS, at : at + 1], (SLOTS, LANES))
                low.append(jnp.where((ids & 127) == lane, 1.0, 0.0).astype(BF))
                high.append((ids >> 7).astype(F32).astype(BF))
            for k in range(blocks):
                k16 = BF(k)
                hot = jnp.where(high[0] == k16, low[0], zero) + jnp.where(
                    high[1] == k16, low[1], zero
                )
                hot_ref[u * SLOTS : (u + 1) * SLOTS, k * LANES : (k + 1) * LANES] = hot
        both = jnp.dot(hot_ref[...], tab_ref[...], preferred_element_type=F32)
        size = GROUP * SLOTS
        found_ref[pl.ds(pl.multiple_of(g * size, size), size), :] = (
            both[:, :LANES] + both[:, LANES:]
        ).astype(BF)

        @pl.when(g > 0)
        def _():
            send_answers(g - 1)

        return carry

    lax.fori_loop(0, PEERS // GROUP, answer_group, 0)
    own_answer.start()
    send_answers(PEERS // GROUP - 1)

    base_ref[:, :, 0:LANES] = dense_ref[...].astype(F32).reshape(samples // 8, 8, LANES)
    labels = jnp.broadcast_to(label_ref[...], (samples, samples)).astype(F32)
    labels = jnp.transpose(labels)[:, 0:1]
    for k in (1, 3, 2):
        for w in range(2):
            across(w, k).wait_recv()
            pass_on(w, k).start()
    own_answer.wait()
    rows_ref[0:SLOTS, :] = ans_ref[0:SLOTS, :].astype(F32)

    def take_answer(j, carry):
        answer_copy(j).wait_recv()
        at = pl.ds(pl.multiple_of(j * SLOTS, SLOTS), SLOTS)
        rows_ref[at, :] = ans_ref[at, :].astype(F32)
        return carry

    lax.fori_loop(1, PEERS, take_answer, 0)
    for copy in to_smem:
        copy.wait()

    def fetch(block, carry):
        b0 = block * 8
        for f in range(features):
            for u in range(8):
                row = rows_ref[pl.ds(pos_s[f, b0 + u], 1), :]
                base_ref[block, u : u + 1, (f + 1) * LANES : (f + 2) * LANES] = row
        return carry

    lax.fori_loop(0, samples // 8, fetch, 0)
    for w in range(2):
        own_weights[w].wait()
        for k in (0, 1, 3, 2):
            pass_on(w, k).wait_recv()
    inputs = base_ref[...].reshape(samples, width).astype(BF)
    crossed = lax.dot_general(inputs, down_ref[...], NT, preferred_element_type=F32).astype(BF)
    base = inputs.astype(F32)
    head = head_ref[...]
    factor = jnp.dot(crossed, up_ref[...], preferred_element_type=F32) + bias_ref[...]
    factor_ref[...] = factor
    logits = jnp.sum((base * factor + base) * head, axis=1, keepdims=True)
    logit_ref[...] = logits
    signal = loss_scale * (jax.nn.sigmoid(logits) - labels)
    state = signal * head
    lift = (state * base).astype(BF)
    cross = lax.dot_general(lift, up_ref[...], NT, preferred_element_type=F32).astype(BF)
    back = state + jnp.dot(cross, down_ref[...], preferred_element_type=F32) + state * factor_ref[...]
    for f in range(features):
        back_ref[f * samples : (f + 1) * samples, :] = back[:, (f + 1) * LANES : (f + 2) * LANES]

    def grad_copy(j):
        return pltpu.make_async_remote_copy(
            src_ref=gsend_ref.at[j], dst_ref=grecv_ref.at[j, pl.ds(0, SLOTS)],
            send_sem=g_send.at[j], recv_sem=g_recv.at[j],
            device_id=(shifted(j, table_at, 1), dp_at), device_id_type=MESH,
        )

    def place(i, carry):
        j = PEERS - 1 - i
        for r in range(SLOTS):
            stage_ref[r : r + 1, :] = back_ref[pl.ds(inv_s[j, r], 1), :]
        gsend_ref[j] = stage_ref[...].astype(BF)

        @pl.when(i > 0)
        def _():
            grad_copy(j + 1).start()

        return carry

    lax.fori_loop(0, PEERS, place, 0)
    own_grad = pltpu.make_async_copy(gsend_ref.at[0], grecv_ref.at[0, pl.ds(0, SLOTS)], l_sem.at[6])
    own_grad.start()

    spot = lax.broadcasted_iota(jnp.int32, (LANES, LANES), 0)
    nothing = jnp.zeros((LANES, LANES), BF)

    def hot_rows(j, u):
        both = asked_ref[j]
        low, high = [], []
        for q in range(2):
            ids = both[q : q + 1, :]
            low.append(jnp.where((ids & 127) == spot, 1.0, 0.0).astype(BF))
            wide = jnp.broadcast_to((ids >> 7).astype(F32), (LANES, LANES))
            high.append(wide.astype(BF))
        for k in range(blocks):
            k16 = BF(k)
            hot = jnp.where(high[0] == k16, low[0], nothing) + jnp.where(
                high[1] == k16, low[1], nothing
            )
            hot2_ref[k * LANES : (k + 1) * LANES, u * LANES : (u + 1) * LANES] = hot

    def take_group(i, carry):
        g = PEERS // GROUP - 1 - i
        for u in range(GROUP):
            hot_rows(g * GROUP + u, u)
        for u in range(GROUP - 1, -1, -1):
            j = g * GROUP + u
            if u == 0:

                @pl.when(j > 0)
                def _():
                    grad_copy(j).wait_recv()

            else:
                grad_copy(j).wait_recv()

        @pl.when(g == 0)
        def _():
            own_grad.wait()

        grads = grecv_ref[pl.ds(pl.multiple_of(g * GROUP, GROUP), GROUP)]
        grads = grads.reshape(GROUP * LANES, LANES)
        acc_ref[...] += jnp.dot(hot2_ref[...], grads, preferred_element_type=F32)
        return carry

    lax.fori_loop(0, PEERS // GROUP, take_group, 0)

    rsend_ref[...] = acc_ref[...].astype(BF)
    part_rows = out_ref.shape[0]

    def part_copy(k):
        target = (dp_at + k) % COPIES
        at = pl.ds(pl.multiple_of(target * part_rows, part_rows), part_rows)
        return pltpu.make_async_remote_copy(
            src_ref=rsend_ref.at[at], dst_ref=rrecv_ref.at[k],
            send_sem=r_send.at[k], recv_sem=r_recv.at[k],
            device_id=(table_at, target), device_id_type=MESH,
        )

    for k in (4, 3, 5, 2, 6, 1, 7):
        part_copy(k).start()
    result = acc_ref[pl.ds(pl.multiple_of(dp_at * part_rows, part_rows), part_rows), :]
    for k in (1, 7, 2, 6, 3, 5, 4):
        part_copy(k).wait_recv()
        result = result + rrecv_ref[k].astype(F32)
    out_ref[...] = result

    def drain(j, carry):
        request_copy(j).wait_send()
        answer_copy(j).wait_send()
        grad_copy(j).wait_send()
        return carry

    lax.fori_loop(1, PEERS, drain, 0)
    for w in range(2):
        for k in range(1, chips):
            across(w, k).wait_send()
        for k in range(chips):
            pass_on(w, k).wait_send()
    for k in range(1, COPIES):
        part_copy(k).wait_send()


def vspec():
    return pl.BlockSpec(memory_space=pltpu.VMEM)


def body(
    emb_table, versions, conf_local, conf_version, conf_values, owners, row_local, lengths,
    dense_out, labels, cross_down, cross_up, cross_bias, head_weight,
):
    rows_dev, emb_width = emb_table.shape
    samples, features, slot_count = row_local.shape
    width, shard = cross_down.shape[1:]
    rank = shard * COPIES
    bags = samples * features
    total = PEERS * SLOTS
    DMA = pltpu.SemaphoreType.DMA
    logits, emb_grad = pl.pallas_call(
        step_kernel,
        out_shape=(
            jax.ShapeDtypeStruct((samples, 1), F32),
            jax.ShapeDtypeStruct((rows_dev // COPIES, emb_width), F32),
        ),
        in_specs=[vspec()] * 14,
        out_specs=(vspec(), vspec()),
        scratch_shapes=[
            VM((features * PEERS, samples), BF),
            VM((features * PEERS, 2 * samples), F32),
            VM((PEERS, bags), BF),
            VM((PARTS * SLOTS, bags), BF),
            VM((PEERS, 2, LANES), jnp.int32),
            VM((PEERS, 2, LANES), jnp.int32),
            VM((features, samples), jnp.int32),
            VM((PEERS, LANES), jnp.int32),
            pltpu.SMEM((features, samples), jnp.int32),
            pltpu.SMEM((PEERS, LANES), jnp.int32),
            VM((rows_dev, 2 * LANES), BF),
            VM((GROUP * SLOTS, rows_dev), BF),
            VM((total, LANES), BF),
            VM((total, LANES), BF),
            VM((total, LANES), F32),
            VM((samples // 8, 8, width), F32),
            VM((samples, width), F32),
            VM((bags, LANES), F32),
            VM((rank, width), BF),
            VM((rank, width), BF),
            VM((SLOTS, LANES), F32),
            VM((PEERS, SLOTS, LANES), BF),
            VM((PEERS, LANES, LANES), BF),
            VM((rows_dev, GROUP * LANES), BF),
            VM((rows_dev, LANES), F32),
            VM((rows_dev, LANES), BF),
            VM((COPIES, rows_dev // COPIES, LANES), BF),
            DMA((PEERS,)), DMA((PEERS,)), DMA((PEERS,)), DMA((PEERS,)), DMA((PEERS,)), DMA((PEERS,)),
            DMA((2, 4)), DMA((2, 4)), DMA((2, 4)), DMA((2, 4)),
            DMA((COPIES,)), DMA((COPIES,)),
            DMA((7,)),
        ],
        compiler_params=pltpu.CompilerParams(
            collective_id=0, has_side_effects=True, vmem_limit_bytes=60 * 1024 * 1024
        ),
        name="step",
    )(
        owners.reshape(samples, features).T,
        jnp.transpose(row_local, (1, 2, 0)),
        lengths.T,
        versions.reshape(1, -1),
        conf_local.reshape(1, -1),
        conf_version.reshape(1, -1),
        emb_table,
        conf_values,
        dense_out,
        labels.reshape(1, -1),
        cross_down[0].T,
        cross_up[0],
        cross_bias,
        head_weight.reshape(1, -1),
    )
    return (logits.reshape(samples), emb_grad)


def solution(mesh):
    in_specs = (
        P("table", None),
        P("table"),
        P("table"),
        P("table"),
        P("table", None),
        P(("table", "dp"), None, None),
        P(("table", "dp"), None, None),
        P(("table", "dp"), None),
        P(("table", "dp"), None),
        P(("table", "dp")),
        P(None, None, "dp"),
        P(None, "dp", None),
        P(),
        P(),
    )
    out_specs = (P(("table", "dp")), P(("table", "dp"), None))
    return jax.shard_map(body, mesh=mesh, in_specs=in_specs, out_specs=out_specs, check_vma=False)
```

```python
import jax
import jax.numpy as jnp
from jax import lax
from jax.experimental import pallas as pl
from jax.experimental.pallas import tpu as pltpu
from jax.sharding import PartitionSpec as P

loss_scale = 64.0
PEERS = 64
COPIES = 8
RING_Y = 4
RING_Z = 16
SLOTS = 80
SENT = 78
ASK = 4
LANES = 128
GROUP = 8
DEAD = 2048
PARTS = 7
VM = pltpu.VMEM
MESH = pl.DeviceIdType.MESH
NT = (((1,), (1,)), ((), ()))
BF = jnp.bfloat16
F32 = jnp.float32


def offset_of(j):
    t = j % RING_Z
    half = (t + 1) // 2
    odd = t % 2
    return j // RING_Z, odd * half + (1 - odd) * (RING_Z - half)


def shifted(j, here, sign):
    dy, dz = offset_of(j)
    y = (here // RING_Z + RING_Y + sign * dy) % RING_Y
    z = (here % RING_Z + 2 * RING_Z + sign * dz) % RING_Z
    return y * RING_Z + z


def slot_of_owner(own, here):
    dy = (own // RING_Z - here // RING_Z + RING_Y) & (RING_Y - 1)
    dz = (own % RING_Z - here % RING_Z + RING_Z) & (RING_Z - 1)
    t = jnp.where(dz == 0, 0, jnp.where(dz <= RING_Z // 2, 2 * dz - 1, 2 * (RING_Z - dz)))
    return dy * RING_Z + t


def step_kernel(
    own_ref, row_ref, len_ref, ver_ref, loc_ref, cver_ref, table_hbm, conf_hbm,
    dense_ref, label_ref, downl_ref, upl_ref, bias_ref, heads_ref,
    logit_ref, out_ref,
    own_s, head_ref, table_ref, conf_ref, hits_ref, prior_ref, wide_ref, placed_ref, req_ref, asked_ref, pos_v, inv_v, pos_s, inv_s,
    tab_ref, hot_ref, found_ref, ans_ref, rows_ref, base_ref, factor_ref, back_ref,
    down_ref, up_ref, stage_ref, gsend_ref, grecv_ref, hot2_ref, acc_ref, rsend_ref, rrecv_ref,
    q_send, q_recv, a_send, a_recv, g_send, g_recv, w_send, w_recv, c_send, c_recv, r_send, r_recv,
    l_sem,
):
    table_at = lax.axis_index("table")
    dp_at = lax.axis_index("dp")
    features, samples = len_ref.shape
    total = PEERS * SLOTS
    width = bias_ref.shape[1]
    shard = downl_ref.shape[0]
    blocks = table_ref.shape[0] // LANES

    barrier = pltpu.get_barrier_semaphore()

    def greet(j, carry):
        pl.semaphore_signal(
            barrier, inc=1, device_id=(shifted(j, table_at, 1), dp_at), device_id_type=MESH
        )
        return carry

    lax.fori_loop(1, PEERS, greet, 0)
    loads = [
        pltpu.make_async_copy(table_hbm, table_ref, l_sem.at[7]),
        pltpu.make_async_copy(conf_hbm, conf_ref, l_sem.at[8]),
    ]
    for load in loads:
        load.start()
    for k in range(1, COPIES):
        pl.semaphore_signal(
            barrier, inc=1, device_id=(table_at, (dp_at + k) % COPIES), device_id_type=MESH
        )

    grecv_ref[:, SENT:LANES, :] = jnp.zeros((PEERS, LANES - SENT, LANES), BF)
    own_s[...] = slot_of_owner(own_ref[:, 0, :], table_at)

    holder = lax.broadcasted_iota(jnp.int32, (PEERS, samples), 0)

    def mark_hits(f, carry):
        hit = jnp.where(own_s[pl.ds(f, 1), :] == holder, 1.0, 0.0).astype(BF)
        hits_ref[pl.ds(pl.multiple_of(f * PEERS, PEERS), PEERS), :] = hit
        wide_ref[:, pl.ds(pl.multiple_of(f * LANES, LANES), LANES)] = hit
        return carry

    lax.fori_loop(0, features, mark_hits, 0, unroll=13)
    row_at = lax.broadcasted_iota(jnp.int32, (samples, 2 * samples), 0)
    col_at = lax.broadcasted_iota(jnp.int32, (samples, 2 * samples), 1)
    before = jnp.where((row_at < col_at) | (col_at >= samples), 1.0, 0.0).astype(BF)
    prior_ref[...] = jnp.dot(hits_ref[...], before, preferred_element_type=F32)
    slot = lax.broadcasted_iota(jnp.int32, (SLOTS, samples), 0).astype(F32)
    sample = lax.broadcasted_iota(jnp.int32, (1, samples), 1).astype(F32)

    def rank_bags(f, carry):
        at = pl.ds(pl.multiple_of(f * PEERS, PEERS), PEERS)
        onehot = hits_ref[at, :].astype(F32)
        rank = jnp.sum(onehot * (prior_ref[at, 0:samples] + carry), axis=0, keepdims=True)
        owner = own_s[pl.ds(f, 1), :]
        pos_v[pl.ds(f, 1), :] = owner * SLOTS + jnp.clip(rank.astype(jnp.int32), 0, SLOTS - 1)
        both = row_ref[f]
        first = both[0:1, :]
        second = jnp.where(len_ref[pl.ds(f, 1), :] > 1, both[1:2, :], DEAD)
        here = slot == rank
        lanes = pl.ds(pl.multiple_of(f * LANES, LANES), LANES)
        values = []
        for value in (first, second):
            values.append((value >> 7).astype(F32))
            values.append((value & 127).astype(F32))
        values.append(jnp.full((1, samples), f, jnp.int32).astype(F32))
        values.append(sample)
        values.append(jnp.ones((1, samples), F32))
        for p, value in enumerate(values):
            placed = jnp.where(here, value, 0.0).astype(BF)
            placed_ref[p * SLOTS : (p + 1) * SLOTS, lanes] = placed
        return carry + prior_ref[at, samples : 2 * samples]

    lax.fori_loop(0, features, rank_bags, jnp.zeros((PEERS, samples), F32), unroll=13)
    packed = lax.dot_general(wide_ref[...], placed_ref[...], NT, preferred_element_type=F32)
    part = [packed[:, p * SLOTS : (p + 1) * SLOTS] for p in range(PARTS)]
    filled = part[6] > 0.5
    dead_tail = jnp.full((PEERS, LANES - SLOTS), DEAD, jnp.int32)
    for q in range(2):
        ids = (part[2 * q] * 128.0 + part[2 * q + 1]).astype(jnp.int32)
        ids = jnp.where(filled, ids, DEAD)
        req_ref[:, q, :] = jnp.concatenate([ids, dead_tail], axis=1)
    inverse = (part[4] * 128.0 + part[5]).astype(jnp.int32)
    inverse = jnp.clip(inverse, 0, features * samples - 1)
    inv_v[...] = jnp.concatenate([inverse, jnp.zeros_like(dead_tail)], axis=1)

    to_smem = [
        pltpu.make_async_copy(pos_v, pos_s, l_sem.at[0]),
        pltpu.make_async_copy(inv_v, inv_s, l_sem.at[1]),
    ]
    for copy in to_smem:
        copy.start()
    own_request = pltpu.make_async_copy(req_ref.at[0], asked_ref.at[0], l_sem.at[2])
    own_request.start()

    pl.semaphore_wait(barrier, PEERS - 1 + COPIES - 1)

    def request_copy(j):
        return pltpu.make_async_remote_copy(
            src_ref=req_ref.at[j], dst_ref=asked_ref.at[j],
            send_sem=q_send.at[j], recv_sem=q_recv.at[j],
            device_id=(shifted(j, table_at, 1), dp_at), device_id_type=MESH,
        )

    def send_request(j, carry):
        request_copy(j).start()
        return carry

    lax.fori_loop(1, PEERS, send_request, 0)

    core, chip = dp_at % 2, dp_at // 2
    chips = COPIES // 2
    weights = ((downl_ref, down_ref), (upl_ref, up_ref))

    def shard_rows(d):
        return pl.ds(pl.multiple_of(d * shard, shard), shard)

    def across(w, k):
        local, full = weights[w]
        return pltpu.make_async_remote_copy(
            src_ref=local, dst_ref=full.at[shard_rows(dp_at)],
            send_sem=w_send.at[w, k], recv_sem=w_recv.at[w, k],
            device_id=(table_at, ((chip + k) % chips) * 2 + core), device_id_type=MESH,
        )

    def pass_on(w, k):
        local, full = weights[w]
        rows = shard_rows(((chip - k + chips) % chips) * 2 + core)
        return pltpu.make_async_remote_copy(
            src_ref=local if k == 0 else full.at[rows], dst_ref=full.at[rows],
            send_sem=c_send.at[w, k], recv_sem=c_recv.at[w, k],
            device_id=(table_at, chip * 2 + 1 - core), device_id_type=MESH,
        )

    own_weights = []
    for w in range(2):
        for k in (1, 3, 2):
            across(w, k).start()
        pass_on(w, 0).start()
        copy = pltpu.make_async_copy(
            weights[w][0], weights[w][1].at[shard_rows(dp_at)], l_sem.at[3 + w]
        )
        copy.start()
        own_weights.append(copy)

    confs = conf_ref.shape[0]
    versions = ver_ref[...]
    pair = jnp.concatenate(
        [(versions >> 7).astype(F32), (versions & 127).astype(F32)]
        + [jnp.zeros((6, versions.shape[1]), F32)], axis=0,
    ).astype(BF)
    local = loc_ref[...]
    line = lax.broadcasted_iota(jnp.int32, (LANES, confs), 0)

    def seen(k, carry):
        hit = jnp.where(line + k * LANES == local, 1.0, 0.0).astype(BF)
        hot2_ref[pl.ds(pl.multiple_of(k * LANES, LANES), LANES), 0:confs] = hit
        return carry

    lax.fori_loop(0, blocks, seen, 0)
    for load in loads:
        load.wait()
    current = jnp.dot(pair, hot2_ref[:, 0:confs], preferred_element_type=F32)
    current = current[0:1, :] * 128.0 + current[1:2, :]
    newer = jnp.where(cver_ref[...].astype(F32) > current, 1.0, 0.0)
    conf = conf_ref[...]
    conf_high = conf.astype(BF)
    conf_low = (conf - conf_high.astype(F32)).astype(BF)
    fresh = jnp.concatenate([conf_high, conf_low, jnp.ones((confs, LANES), BF)], axis=1)

    def renew(k, carry):
        at = pl.ds(pl.multiple_of(k * LANES, LANES), LANES)
        mask = (hot2_ref[at, 0:confs].astype(F32) * newer).astype(BF)
        got = jnp.dot(mask, fresh, preferred_element_type=F32)
        now = table_ref[at, :]
        high = now.astype(BF).astype(F32)
        take = got[:, 2 * LANES : 3 * LANES] > 0.5
        tab_ref[at, 0:LANES] = jnp.where(take, got[:, 0:LANES], high).astype(BF)
        low = jnp.where(take, got[:, LANES : 2 * LANES], now - high)
        tab_ref[at, LANES : 2 * LANES] = low.astype(BF)
        return carry

    lax.fori_loop(0, blocks, renew, 0)

    own_request.wait()
    lane = lax.broadcasted_iota(jnp.int32, (SLOTS, LANES), 1)
    zero = jnp.zeros((SLOTS, LANES), BF)

    def chunk(ref, j):
        return ref.at[pl.ds(pl.multiple_of(j * SLOTS, SLOTS), SENT)]

    def group_at(i):
        late = (i + 3) // 8
        return (1 - late) * (2 * i - 1) + late * (16 - 2 * i) + (8 - i) // 8

    def answer_copy(j):
        return pltpu.make_async_remote_copy(
            src_ref=chunk(found_ref, j), dst_ref=chunk(ans_ref, j),
            send_sem=a_send.at[j], recv_sem=a_recv.at[j],
            device_id=(shifted(j, table_at, -1), dp_at), device_id_type=MESH,
        )

    own_answer = pltpu.make_async_copy(
        found_ref.at[0:SENT], ans_ref.at[0:SENT], l_sem.at[5]
    )

    def first_slot(i):
        per = GROUP // ASK
        return group_at(i // per) * GROUP + (i % per) * ASK

    def send_answers(i):
        start = first_slot(i)

        @pl.when(i > 0)
        def _():
            answer_copy(start).start()

        for u in range(1, ASK):
            answer_copy(start + u).start()

    def answer_group(i, carry):
        start = first_slot(i)

        @pl.when(i > 0)
        def _():
            request_copy(start).wait_recv()

        for u in range(1, ASK):
            request_copy(start + u).wait_recv()
        columns = jnp.transpose(
            jnp.concatenate([asked_ref[start + u] for u in range(ASK)], axis=0)
        )
        for u in range(ASK):
            low, high = [], []
            for q in range(2):
                at = 2 * u + q
                ids = jnp.broadcast_to(columns[0:SLOTS, at : at + 1], (SLOTS, LANES))
                low.append(jnp.where((ids & 127) == lane, 1.0, 0.0).astype(BF))
                high.append((ids >> 7).astype(F32).astype(BF))
            for k in range(blocks):
                k16 = BF(k)
                hot = jnp.where(high[0] == k16, low[0], zero) + jnp.where(
                    high[1] == k16, low[1], zero
                )
                hot_ref[u * SLOTS : (u + 1) * SLOTS, k * LANES : (k + 1) * LANES] = hot
        both = jnp.dot(hot_ref[...], tab_ref[...], preferred_element_type=F32)
        found_ref[pl.ds(pl.multiple_of(start * SLOTS, SLOTS), ASK * SLOTS), :] = (
            both[:, :LANES] + both[:, LANES:]
        ).astype(BF)

        @pl.when(i > 0)
        def _():
            send_answers(i - 1)

        return carry

    lax.fori_loop(0, PEERS // ASK, answer_group, 0)
    own_answer.start()
    send_answers(jnp.int32(PEERS // ASK - 1))

    acc_ref[...] = jnp.zeros_like(acc_ref)
    for f in range(features + 1):
        head_ref[:, f * LANES : (f + 1) * LANES] = heads_ref[f : f + 1, :]
    base_ref[:, :, 0:LANES] = dense_ref[...].astype(F32).reshape(samples // 8, 8, LANES)
    labels = jnp.broadcast_to(label_ref[...], (samples, samples)).astype(F32)
    labels = jnp.transpose(labels)[:, 0:1]
    for k in (1, 3, 2):
        for w in range(2):
            across(w, k).wait_recv()
            pass_on(w, k).start()
    own_answer.wait()
    rows_ref[0:SLOTS, :] = ans_ref[0:SLOTS, :].astype(F32)

    def take_answer(j, carry):
        answer_copy(j).wait_recv()
        at = pl.ds(pl.multiple_of(j * SLOTS, SLOTS), SLOTS)
        rows_ref[at, :] = ans_ref[at, :].astype(F32)
        return carry

    lax.fori_loop(1, PEERS, take_answer, 0)
    for copy in to_smem:
        copy.wait()

    def fetch(block, carry):
        b0 = block * 8
        for f in range(features):
            for u in range(8):
                row = rows_ref[pl.ds(pos_s[f, b0 + u], 1), :]
                base_ref[block, u : u + 1, (f + 1) * LANES : (f + 2) * LANES] = row
        return carry

    lax.fori_loop(0, samples // 8, fetch, 0)
    for w in range(2):
        own_weights[w].wait()
        for k in (0, 1, 3, 2):
            pass_on(w, k).wait_recv()
    inputs = base_ref[...].reshape(samples, width).astype(BF)
    crossed = lax.dot_general(inputs, down_ref[...], NT, preferred_element_type=F32).astype(BF)
    base = inputs.astype(F32)
    head = head_ref[...]
    factor = jnp.dot(crossed, up_ref[...], preferred_element_type=F32) + bias_ref[...]
    factor_ref[...] = factor
    logits = jnp.sum((base * factor + base) * head, axis=1, keepdims=True)
    logit_ref[...] = jnp.transpose(jnp.broadcast_to(logits, (samples, samples)))[0:1, :]
    signal = loss_scale * (jax.nn.sigmoid(logits) - labels)
    state = signal * head
    lift = (state * base).astype(BF)
    cross = lax.dot_general(lift, up_ref[...], NT, preferred_element_type=F32).astype(BF)
    back = state + jnp.dot(cross, down_ref[...], preferred_element_type=F32) + state * factor_ref[...]
    for f in range(features):
        back_ref[f * samples : (f + 1) * samples, :] = back[:, (f + 1) * LANES : (f + 2) * LANES]

    def grad_copy(j):
        return pltpu.make_async_remote_copy(
            src_ref=gsend_ref.at[j, pl.ds(0, SENT)], dst_ref=grecv_ref.at[j, pl.ds(0, SENT)],
            send_sem=g_send.at[j], recv_sem=g_recv.at[j],
            device_id=(shifted(j, table_at, 1), dp_at), device_id_type=MESH,
        )

    def place(i, carry):
        j = PEERS - 1 - i
        for r in range(SLOTS):
            stage_ref[r : r + 1, :] = back_ref[pl.ds(inv_s[j, r], 1), :]
        gsend_ref[j] = stage_ref[...].astype(BF)

        @pl.when(i > 0)
        def _():
            grad_copy(j + 1).start()

        return carry

    lax.fori_loop(0, PEERS, place, 0)
    own_grad = pltpu.make_async_copy(
        gsend_ref.at[0, pl.ds(0, SENT)], grecv_ref.at[0, pl.ds(0, SENT)], l_sem.at[6]
    )
    own_grad.start()

    spot = lax.broadcasted_iota(jnp.int32, (LANES, LANES), 0)
    nothing = jnp.zeros((LANES, LANES), BF)

    def hot_rows(j, u):
        both = asked_ref[j]
        low, high = [], []
        for q in range(2):
            ids = both[q : q + 1, :]
            low.append(jnp.where((ids & 127) == spot, 1.0, 0.0).astype(BF))
            wide = jnp.broadcast_to((ids >> 7).astype(F32), (LANES, LANES))
            high.append(wide.astype(BF))
        for k in range(blocks):
            k16 = BF(k)
            hot = jnp.where(high[0] == k16, low[0], nothing) + jnp.where(
                high[1] == k16, low[1], nothing
            )
            hot2_ref[k * LANES : (k + 1) * LANES, u * LANES : (u + 1) * LANES] = hot

    def grads_of(g):
        for u in range(GROUP):
            hot_rows(g * GROUP + u, u)
        for u in range(GROUP - 1, 0, -1):
            grad_copy(g * GROUP + u).wait_recv()

    def group_rows(g):
        grads = grecv_ref[pl.ds(pl.multiple_of(g * GROUP, GROUP), GROUP)]
        return grads.reshape(GROUP * LANES, LANES)

    def take_group(i, carry):
        g = PEERS // GROUP - 1 - i
        grads_of(g)
        grad_copy(g * GROUP).wait_recv()
        acc_ref[...] += jnp.dot(hot2_ref[...], group_rows(g), preferred_element_type=F32)
        return carry

    lax.fori_loop(0, PEERS // GROUP - 1, take_group, 0)
    grads_of(0)
    own_grad.wait()

    part_rows = out_ref.shape[0]
    last = grecv_ref[0:GROUP].reshape(GROUP * LANES, LANES)

    def part_at(k):
        target = (dp_at + k) % COPIES
        return pl.ds(pl.multiple_of(target * part_rows, part_rows), part_rows)

    def part_copy(k):
        return pltpu.make_async_remote_copy(
            src_ref=rsend_ref.at[part_at(k)], dst_ref=rrecv_ref.at[k],
            send_sem=r_send.at[k], recv_sem=r_recv.at[k],
            device_id=(table_at, (dp_at + k) % COPIES), device_id_type=MESH,
        )

    def part_sum(k):
        at = part_at(k)
        return acc_ref[at, :] + jnp.dot(hot2_ref[at, :], last, preferred_element_type=F32)

    order = (4, 3, 5, 2, 6, 1, 7)
    for n, k in enumerate(order):
        rsend_ref[part_at(k), :] = part_sum(k).astype(BF)
        if n > 0:
            part_copy(order[n - 1]).start()
    result = part_sum(0)
    part_copy(order[-1]).start()
    for k in (1, 7, 2, 6, 3, 5, 4):
        part_copy(k).wait_recv()
        result = result + rrecv_ref[k].astype(F32)
    out_ref[...] = result

    def drain(j, carry):
        request_copy(j).wait_send()
        answer_copy(j).wait_send()
        grad_copy(j).wait_send()
        return carry

    lax.fori_loop(1, PEERS, drain, 0)
    for w in range(2):
        for k in range(1, chips):
            across(w, k).wait_send()
        for k in range(chips):
            pass_on(w, k).wait_send()
    for k in range(1, COPIES):
        part_copy(k).wait_send()


def vspec():
    return pl.BlockSpec(memory_space=pltpu.VMEM)


def body(
    emb_table, versions, conf_local, conf_version, conf_values, owners, row_local, lengths,
    dense_out, labels, cross_down, cross_up, cross_bias, head_weight,
):
    rows_dev, emb_width = emb_table.shape
    samples, features, slot_count = row_local.shape
    width, shard = cross_down.shape[1:]
    rank = shard * COPIES
    bags = samples * features
    total = PEERS * SLOTS
    DMA = pltpu.SemaphoreType.DMA
    hbm = pl.BlockSpec(memory_space=pl.ANY)
    logits, emb_grad = pl.pallas_call(
        step_kernel,
        out_shape=(
            jax.ShapeDtypeStruct((1, samples), F32),
            jax.ShapeDtypeStruct((rows_dev // COPIES, emb_width), F32),
        ),
        in_specs=[vspec()] * 6 + [hbm, hbm] + [vspec()] * 2 + [hbm, hbm] + [vspec()] * 2,
        out_specs=(vspec(), vspec()),
        scratch_shapes=[
            VM((features, samples), jnp.int32),
            VM((1, width), F32),
            VM((rows_dev, LANES), F32),
            VM((conf_local.shape[0], LANES), F32),
            VM((features * PEERS, samples), BF),
            VM((features * PEERS, 2 * samples), F32),
            VM((PEERS, bags), BF),
            VM((PARTS * SLOTS, bags), BF),
            VM((PEERS, 2, LANES), jnp.int32),
            VM((PEERS, 2, LANES), jnp.int32),
            VM((features, samples), jnp.int32),
            VM((PEERS, LANES), jnp.int32),
            pltpu.SMEM((features, samples), jnp.int32),
            pltpu.SMEM((PEERS, LANES), jnp.int32),
            VM((rows_dev, 2 * LANES), BF),
            VM((ASK * SLOTS, rows_dev), BF),
            VM((total, LANES), BF),
            VM((total, LANES), BF),
            VM((total, LANES), F32),
            VM((samples // 8, 8, width), F32),
            VM((samples, width), F32),
            VM((bags, LANES), F32),
            VM((rank, width), BF),
            VM((rank, width), BF),
            VM((SLOTS, LANES), F32),
            VM((PEERS, SLOTS, LANES), BF),
            VM((PEERS, LANES, LANES), BF),
            VM((rows_dev, GROUP * LANES), BF),
            VM((rows_dev, LANES), F32),
            VM((rows_dev, LANES), BF),
            VM((COPIES, rows_dev // COPIES, LANES), BF),
            DMA((PEERS,)), DMA((PEERS,)), DMA((PEERS,)), DMA((PEERS,)), DMA((PEERS,)), DMA((PEERS,)),
            DMA((2, 4)), DMA((2, 4)), DMA((2, 4)), DMA((2, 4)),
            DMA((COPIES,)), DMA((COPIES,)),
            DMA((9,)),
        ],
        compiler_params=pltpu.CompilerParams(
            collective_id=0, has_side_effects=True, vmem_limit_bytes=60 * 1024 * 1024
        ),
        name="step",
    )(
        jnp.transpose(owners, (1, 2, 0)),
        jnp.transpose(row_local, (1, 2, 0)),
        lengths.T,
        versions.reshape(1, -1),
        conf_local.reshape(1, -1),
        conf_version.reshape(1, -1),
        emb_table,
        conf_values,
        dense_out,
        labels.reshape(1, -1),
        cross_down[0].T,
        cross_up[0],
        cross_bias,
        head_weight.reshape(-1, LANES),
    )
    return (logits.reshape(samples), emb_grad)


def solution(mesh):
    in_specs = (
        P("table", None),
        P("table"),
        P("table"),
        P("table"),
        P("table", None),
        P(("table", "dp"), None, None),
        P(("table", "dp"), None, None),
        P(("table", "dp"), None),
        P(("table", "dp"), None),
        P(("table", "dp")),
        P(None, None, "dp"),
        P(None, "dp", None),
        P(),
        P(),
    )
    out_specs = (P(("table", "dp")), P(("table", "dp"), None))
    return jax.shard_map(body, mesh=mesh, in_specs=in_specs, out_specs=out_specs, check_vma=False)
```

```python
import jax
import jax.numpy as jnp
from jax import lax
from jax.experimental import pallas as pl
from jax.experimental.pallas import tpu as pltpu
from jax.sharding import PartitionSpec as P

loss_scale = 64.0
PEERS = 64
COPIES = 8
RING_Y = 4
RING_Z = 16
SLOTS = 80
SENT = 78
ASK = 2
LANES = 128
GROUP = 8
DEAD = 2048
PARTS = 7
VM = pltpu.VMEM
MESH = pl.DeviceIdType.MESH
NT = (((1,), (1,)), ((), ()))
BF = jnp.bfloat16
F32 = jnp.float32


def offset_of(j):
    t = j % RING_Z
    half = (t + 1) // 2
    odd = t % 2
    return j // RING_Z, odd * half + (1 - odd) * (RING_Z - half)


def shifted(j, here, sign):
    dy, dz = offset_of(j)
    y = (here // RING_Z + RING_Y + sign * dy) % RING_Y
    z = (here % RING_Z + 2 * RING_Z + sign * dz) % RING_Z
    return y * RING_Z + z


def slot_of_owner(own, here):
    dy = (own // RING_Z - here // RING_Z + RING_Y) & (RING_Y - 1)
    dz = (own % RING_Z - here % RING_Z + RING_Z) & (RING_Z - 1)
    t = jnp.where(dz == 0, 0, jnp.where(dz <= RING_Z // 2, 2 * dz - 1, 2 * (RING_Z - dz)))
    return dy * RING_Z + t


def step_kernel(
    own_hbm, row_hbm, len_hbm, ver_hbm, loc_hbm, cver_hbm, table_hbm, conf_hbm,
    dense_hbm, label_hbm, downl_ref, upl_ref, bias_hbm, heads_hbm,
    logit_ref, out_ref,
    own_ref, row_ref, len_ref, ver_ref, loc_ref, cver_ref, dense_ref, label_ref, bias_ref, heads_ref,
    own_s, head_ref, table_ref, conf_ref, hits_ref, prior_ref, wide_ref, placed_ref, req_ref, asked_ref, pos_v, inv_v, pos_s, inv_s,
    tab_ref, hot_ref, found_ref, ans_ref, rows_ref, base_ref, factor_ref, back_ref,
    down_ref, up_ref, stage_ref, gsend_ref, grecv_ref, hot2_ref, acc_ref, rown_ref, rsend_ref, rrecv_ref,
    q_send, q_recv, a_send, a_recv, g_send, g_recv, w_send, w_recv, c_send, c_recv, r_send, r_recv,
    l_sem,
):
    table_at = lax.axis_index("table")
    dp_at = lax.axis_index("dp")
    features, samples = len_hbm.shape
    total = PEERS * SLOTS
    width = bias_ref.shape[1]
    shard = downl_ref.shape[0]
    blocks = table_ref.shape[0] // LANES

    barrier = pltpu.get_barrier_semaphore()

    def greet(i, carry):
        pl.semaphore_signal(
            barrier, inc=1, device_id=(shifted(PEERS - i, table_at, 1), dp_at), device_id_type=MESH
        )
        return carry

    lax.fori_loop(1, PEERS, greet, 0)
    core, chip = dp_at % 2, dp_at // 2
    chips = COPIES // 2
    for k in range(1, chips):
        pl.semaphore_signal(
            barrier, inc=1, device_id=(table_at, ((chip + k) % chips) * 2 + core),
            device_id_type=MESH,
        )
    pl.semaphore_signal(
        barrier, inc=1, device_id=(table_at, chip * 2 + 1 - core), device_id_type=MESH
    )
    sources = (
        (own_hbm, own_ref), (row_hbm, row_ref), (len_hbm, len_ref), (ver_hbm, ver_ref),
        (loc_hbm, loc_ref), (cver_hbm, cver_ref), (dense_hbm, dense_ref), (label_hbm, label_ref),
        (bias_hbm, bias_ref), (heads_hbm, heads_ref), (table_hbm, table_ref), (conf_hbm, conf_ref),
    )
    loads = [
        pltpu.make_async_copy(src, dst, l_sem.at[7 + n]) for n, (src, dst) in enumerate(sources)
    ]
    for load in loads:
        load.start()
    grecv_ref[:, SENT:LANES, :] = jnp.zeros((PEERS, LANES - SENT, LANES), BF)
    for load in loads[:3]:
        load.wait()
    own_s[...] = slot_of_owner(own_ref[:, 0, :], table_at)

    holder = lax.broadcasted_iota(jnp.int32, (PEERS, samples), 0)

    def mark_hits(f, carry):
        hit = jnp.where(own_s[pl.ds(f, 1), :] == holder, 1.0, 0.0).astype(BF)
        hits_ref[pl.ds(pl.multiple_of(f * PEERS, PEERS), PEERS), :] = hit
        wide_ref[:, pl.ds(pl.multiple_of(f * LANES, LANES), LANES)] = hit
        return carry

    lax.fori_loop(0, features, mark_hits, 0, unroll=13)
    row_at = lax.broadcasted_iota(jnp.int32, (samples, 2 * samples), 0)
    col_at = lax.broadcasted_iota(jnp.int32, (samples, 2 * samples), 1)
    before = jnp.where((row_at < col_at) | (col_at >= samples), 1.0, 0.0).astype(BF)
    prior_ref[...] = jnp.dot(hits_ref[...], before, preferred_element_type=F32)
    slot = lax.broadcasted_iota(jnp.int32, (SLOTS, samples), 0).astype(F32)
    sample = lax.broadcasted_iota(jnp.int32, (1, samples), 1).astype(F32)

    def rank_bags(f, carry):
        at = pl.ds(pl.multiple_of(f * PEERS, PEERS), PEERS)
        onehot = hits_ref[at, :].astype(F32)
        rank = jnp.sum(onehot * (prior_ref[at, 0:samples] + carry), axis=0, keepdims=True)
        owner = own_s[pl.ds(f, 1), :]
        pos_v[pl.ds(f, 1), :] = owner * SLOTS + jnp.clip(rank.astype(jnp.int32), 0, SLOTS - 1)
        both = row_ref[f]
        first = both[0:1, :]
        second = jnp.where(len_ref[pl.ds(f, 1), :] > 1, both[1:2, :], DEAD)
        here = slot == rank
        lanes = pl.ds(pl.multiple_of(f * LANES, LANES), LANES)
        values = []
        for value in (first, second):
            values.append((value >> 7).astype(F32))
            values.append((value & 127).astype(F32))
        values.append(jnp.full((1, samples), f, jnp.int32).astype(F32))
        values.append(sample)
        values.append(jnp.ones((1, samples), F32))
        for p, value in enumerate(values):
            placed = jnp.where(here, value, 0.0).astype(BF)
            placed_ref[p * SLOTS : (p + 1) * SLOTS, lanes] = placed
        return carry + prior_ref[at, samples : 2 * samples]

    lax.fori_loop(0, features, rank_bags, jnp.zeros((PEERS, samples), F32), unroll=13)
    packed = lax.dot_general(wide_ref[...], placed_ref[...], NT, preferred_element_type=F32)
    part = [packed[:, p * SLOTS : (p + 1) * SLOTS] for p in range(PARTS)]
    filled = part[6] > 0.5
    dead_tail = jnp.full((PEERS, LANES - SLOTS), DEAD, jnp.int32)
    for q in range(2):
        ids = (part[2 * q] * 128.0 + part[2 * q + 1]).astype(jnp.int32)
        ids = jnp.where(filled, ids, DEAD)
        req_ref[:, q, :] = jnp.concatenate([ids, dead_tail], axis=1)
    inverse = (part[4] * 128.0 + part[5]).astype(jnp.int32)
    inverse = jnp.clip(inverse, 0, features * samples - 1)
    inv_v[...] = jnp.concatenate([inverse, jnp.zeros_like(dead_tail)], axis=1)

    to_smem = [
        pltpu.make_async_copy(pos_v, pos_s, l_sem.at[0]),
        pltpu.make_async_copy(inv_v, inv_s, l_sem.at[1]),
    ]
    for copy in to_smem:
        copy.start()
    own_request = pltpu.make_async_copy(req_ref.at[0], asked_ref.at[0], l_sem.at[2])
    own_request.start()

    pl.semaphore_wait(barrier, PEERS - 1 + chips)

    def request_copy(j):
        return pltpu.make_async_remote_copy(
            src_ref=req_ref.at[j], dst_ref=asked_ref.at[j],
            send_sem=q_send.at[j], recv_sem=q_recv.at[j],
            device_id=(shifted(j, table_at, 1), dp_at), device_id_type=MESH,
        )

    def send_request(i, carry):
        request_copy(PEERS - i).start()
        return carry

    lax.fori_loop(1, PEERS, send_request, 0)

    weights = ((downl_ref, down_ref), (upl_ref, up_ref))

    def shard_rows(d):
        return pl.ds(pl.multiple_of(d * shard, shard), shard)

    def across(w, k):
        local, full = weights[w]
        return pltpu.make_async_remote_copy(
            src_ref=local, dst_ref=full.at[shard_rows(dp_at)],
            send_sem=w_send.at[w, k], recv_sem=w_recv.at[w, k],
            device_id=(table_at, ((chip + k) % chips) * 2 + core), device_id_type=MESH,
        )

    def pass_on(w, k):
        local, full = weights[w]
        rows = shard_rows(((chip - k + chips) % chips) * 2 + core)
        return pltpu.make_async_remote_copy(
            src_ref=local if k == 0 else full.at[rows], dst_ref=full.at[rows],
            send_sem=c_send.at[w, k], recv_sem=c_recv.at[w, k],
            device_id=(table_at, chip * 2 + 1 - core), device_id_type=MESH,
        )

    own_weights = []
    for w in range(2):
        for k in (1, 3, 2):
            across(w, k).start()
        pass_on(w, 0).start()
        copy = pltpu.make_async_copy(
            weights[w][0], weights[w][1].at[shard_rows(dp_at)], l_sem.at[3 + w]
        )
        copy.start()
        own_weights.append(copy)

    for load in loads[3:]:
        load.wait()
    confs = conf_ref.shape[0]
    versions = ver_ref[...]
    pair = jnp.concatenate(
        [(versions >> 7).astype(F32), (versions & 127).astype(F32)]
        + [jnp.zeros((6, versions.shape[1]), F32)], axis=0,
    ).astype(BF)
    local = loc_ref[...]
    line = lax.broadcasted_iota(jnp.int32, (LANES, confs), 0)

    def seen(k, carry):
        hit = jnp.where(line + k * LANES == local, 1.0, 0.0).astype(BF)
        hot2_ref[pl.ds(pl.multiple_of(k * LANES, LANES), LANES), 0:confs] = hit
        return carry

    lax.fori_loop(0, blocks, seen, 0)
    current = jnp.dot(pair, hot2_ref[:, 0:confs], preferred_element_type=F32)
    current = current[0:1, :] * 128.0 + current[1:2, :]
    newer = jnp.where(cver_ref[...].astype(F32) > current, 1.0, 0.0)
    conf = conf_ref[...]
    conf_high = conf.astype(BF)
    conf_low = (conf - conf_high.astype(F32)).astype(BF)
    fresh = jnp.concatenate([conf_high, conf_low, jnp.ones((confs, LANES), BF)], axis=1)

    def renew(k, carry):
        at = pl.ds(pl.multiple_of(k * LANES, LANES), LANES)
        mask = (hot2_ref[at, 0:confs].astype(F32) * newer).astype(BF)
        got = jnp.dot(mask, fresh, preferred_element_type=F32)
        now = table_ref[at, :]
        high = now.astype(BF).astype(F32)
        take = got[:, 2 * LANES : 3 * LANES] > 0.5
        tab_ref[at, 0:LANES] = jnp.where(take, got[:, 0:LANES], high).astype(BF)
        low = jnp.where(take, got[:, LANES : 2 * LANES], now - high)
        tab_ref[at, LANES : 2 * LANES] = low.astype(BF)
        return carry

    lax.fori_loop(0, blocks, renew, 0)

    own_request.wait()
    lane = lax.broadcasted_iota(jnp.int32, (SLOTS, LANES), 1)
    zero = jnp.zeros((SLOTS, LANES), BF)

    def chunk(ref, j):
        return ref.at[pl.ds(pl.multiple_of(j * SLOTS, SLOTS), SENT)]

    def group_at(i):
        late = (i + 3) // 8
        return (1 - late) * (2 * i - 1) + late * (16 - 2 * i) + (8 - i) // 8

    def answer_copy(j):
        return pltpu.make_async_remote_copy(
            src_ref=chunk(found_ref, j), dst_ref=chunk(ans_ref, j),
            send_sem=a_send.at[j], recv_sem=a_recv.at[j],
            device_id=(shifted(j, table_at, -1), dp_at), device_id_type=MESH,
        )

    own_answer = pltpu.make_async_copy(
        found_ref.at[0:SENT], ans_ref.at[0:SENT], l_sem.at[5]
    )

    def first_slot(i):
        per = GROUP // ASK
        return group_at(i // per) * GROUP + (i % per) * ASK

    def send_answers(i):
        start = first_slot(i)

        @pl.when(i > 0)
        def _():
            answer_copy(start).start()

        for u in range(1, ASK):
            answer_copy(start + u).start()

    def answer_group(i, carry):
        start = first_slot(i)

        @pl.when(i > 0)
        def _():
            request_copy(start).wait_recv()

        for u in range(1, ASK):
            request_copy(start + u).wait_recv()
        columns = jnp.transpose(
            jnp.concatenate([asked_ref[start + u] for u in range(ASK)], axis=0)
        )
        for u in range(ASK):
            low, high = [], []
            for q in range(2):
                at = 2 * u + q
                ids = jnp.broadcast_to(columns[0:SLOTS, at : at + 1], (SLOTS, LANES))
                low.append(jnp.where((ids & 127) == lane, 1.0, 0.0).astype(BF))
                high.append((ids >> 7).astype(F32).astype(BF))
            for k in range(blocks):
                k16 = BF(k)
                hot = jnp.where(high[0] == k16, low[0], zero) + jnp.where(
                    high[1] == k16, low[1], zero
                )
                hot_ref[u * SLOTS : (u + 1) * SLOTS, k * LANES : (k + 1) * LANES] = hot
        both = jnp.dot(hot_ref[...], tab_ref[...], preferred_element_type=F32)
        found_ref[pl.ds(pl.multiple_of(start * SLOTS, SLOTS), ASK * SLOTS), :] = (
            both[:, :LANES] + both[:, LANES:]
        ).astype(BF)

        @pl.when(i > 0)
        def _():
            send_answers(i - 1)

        return carry

    lax.fori_loop(0, PEERS // ASK, answer_group, 0)
    own_answer.start()
    send_answers(jnp.int32(PEERS // ASK - 1))

    acc_ref[...] = jnp.zeros_like(acc_ref)
    for f in range(features + 1):
        head_ref[:, f * LANES : (f + 1) * LANES] = heads_ref[f : f + 1, :]
    base_ref[:, :, 0:LANES] = dense_ref[...].astype(F32).reshape(samples // 8, 8, LANES)
    labels = jnp.broadcast_to(label_ref[...], (samples, samples)).astype(F32)
    labels = jnp.transpose(labels)[:, 0:1]
    for k in (1, 3, 2):
        for w in range(2):
            across(w, k).wait_recv()
            pass_on(w, k).start()
    own_answer.wait()
    rows_ref[0:SLOTS, :] = ans_ref[0:SLOTS, :].astype(F32)

    def take_answer(j, carry):
        answer_copy(j).wait_recv()
        at = pl.ds(pl.multiple_of(j * SLOTS, SLOTS), SLOTS)
        rows_ref[at, :] = ans_ref[at, :].astype(F32)
        return carry

    lax.fori_loop(1, PEERS, take_answer, 0)
    for copy in to_smem:
        copy.wait()

    def fetch(block, carry):
        b0 = block * 8
        for f in range(features):
            for u in range(8):
                row = rows_ref[pl.ds(pos_s[f, b0 + u], 1), :]
                base_ref[block, u : u + 1, (f + 1) * LANES : (f + 2) * LANES] = row
        return carry

    lax.fori_loop(0, samples // 8, fetch, 0)
    for w in range(2):
        own_weights[w].wait()
        for k in (0, 1, 3, 2):
            pass_on(w, k).wait_recv()
    inputs = base_ref[...].reshape(samples, width).astype(BF)
    crossed = lax.dot_general(inputs, down_ref[...], NT, preferred_element_type=F32).astype(BF)
    base = inputs.astype(F32)
    head = head_ref[...]
    factor = jnp.dot(crossed, up_ref[...], preferred_element_type=F32) + bias_ref[...]
    factor_ref[...] = factor
    logits = jnp.sum((base * factor + base) * head, axis=1, keepdims=True)
    logit_ref[...] = jnp.transpose(jnp.broadcast_to(logits, (samples, samples)))[0, :]
    signal = loss_scale * (jax.nn.sigmoid(logits) - labels)
    state = signal * head
    lift = (state * base).astype(BF)
    cross = lax.dot_general(lift, up_ref[...], NT, preferred_element_type=F32).astype(BF)
    back = state + jnp.dot(cross, down_ref[...], preferred_element_type=F32) + state * factor_ref[...]
    for f in range(features):
        back_ref[f * samples : (f + 1) * samples, :] = back[:, (f + 1) * LANES : (f + 2) * LANES]

    def grad_copy(j):
        return pltpu.make_async_remote_copy(
            src_ref=gsend_ref.at[j, pl.ds(0, SENT)], dst_ref=grecv_ref.at[j, pl.ds(0, SENT)],
            send_sem=g_send.at[j], recv_sem=g_recv.at[j],
            device_id=(shifted(j, table_at, 1), dp_at), device_id_type=MESH,
        )

    def place(i, carry):
        j = PEERS - 1 - i
        for r in range(SLOTS):
            stage_ref[r : r + 1, :] = back_ref[pl.ds(inv_s[j, r], 1), :]
        gsend_ref[j] = stage_ref[...].astype(BF)

        @pl.when(i > 0)
        def _():
            grad_copy(j + 1).start()

        return carry

    lax.fori_loop(0, PEERS, place, 0)
    own_grad = pltpu.make_async_copy(
        gsend_ref.at[0, pl.ds(0, SENT)], grecv_ref.at[0, pl.ds(0, SENT)], l_sem.at[6]
    )
    own_grad.start()

    def drain(j, carry):
        request_copy(j).wait_send()
        answer_copy(j).wait_send()
        return carry

    lax.fori_loop(1, PEERS, drain, 0)
    for w in range(2):
        for k in range(1, chips):
            across(w, k).wait_send()
        for k in range(chips):
            pass_on(w, k).wait_send()

    spot = lax.broadcasted_iota(jnp.int32, (LANES, LANES), 0)
    nothing = jnp.zeros((LANES, LANES), BF)

    def hot_rows(j, u):
        both = asked_ref[j]
        low, high = [], []
        for q in range(2):
            ids = both[q : q + 1, :]
            low.append(jnp.where((ids & 127) == spot, 1.0, 0.0).astype(BF))
            wide = jnp.broadcast_to((ids >> 7).astype(F32), (LANES, LANES))
            high.append(wide.astype(BF))
        for k in range(blocks):
            k16 = BF(k)
            hot = jnp.where(high[0] == k16, low[0], nothing) + jnp.where(
                high[1] == k16, low[1], nothing
            )
            hot2_ref[k * LANES : (k + 1) * LANES, u * LANES : (u + 1) * LANES] = hot

    def grads_of(g):
        for u in range(GROUP):
            hot_rows(g * GROUP + u, u)
        for u in range(GROUP - 1, 0, -1):
            grad_copy(g * GROUP + u).wait_recv()

    def group_rows(g):
        grads = grecv_ref[pl.ds(pl.multiple_of(g * GROUP, GROUP), GROUP)]
        return grads.reshape(GROUP * LANES, LANES)

    def take_group(i, carry):
        g = PEERS // GROUP - 1 - i
        grads_of(g)
        grad_copy(g * GROUP).wait_recv()
        acc_ref[...] += jnp.dot(hot2_ref[...], group_rows(g), preferred_element_type=F32)
        for u in range(GROUP):
            grad_copy(g * GROUP + u).wait_send()
        return carry

    lax.fori_loop(0, PEERS // GROUP - 1, take_group, 0)
    grads_of(0)
    own_grad.wait()

    part_rows = out_ref.shape[0]
    last = grecv_ref[0:GROUP].reshape(GROUP * LANES, LANES)

    def part_at(k, side):
        target = ((chip + k) % chips) * 2 + side
        return pl.ds(pl.multiple_of(target * part_rows, part_rows), part_rows)

    def part_sum(k, side):
        at = part_at(k, side)
        return acc_ref[at, :] + jnp.dot(hot2_ref[at, :], last, preferred_element_type=F32)

    def beside(k):
        return pltpu.make_async_remote_copy(
            src_ref=rsend_ref.at[k], dst_ref=rrecv_ref.at[k],
            send_sem=r_send.at[k], recv_sem=r_recv.at[k],
            device_id=(table_at, chip * 2 + 1 - core), device_id_type=MESH,
        )

    def along(k):
        return pltpu.make_async_remote_copy(
            src_ref=rsend_ref.at[chips + k], dst_ref=rrecv_ref.at[chips + k],
            send_sem=r_send.at[chips + k], recv_sem=r_recv.at[chips + k],
            device_id=(table_at, ((chip + k) % chips) * 2 + core), device_id_type=MESH,
        )

    order = (2, 3, 1, 0)
    for n, k in enumerate(order):
        rsend_ref[k] = part_sum(k, 1 - core).astype(BF)
        if n > 0:
            beside(order[n - 1]).start()
    for n, k in enumerate(order):
        rown_ref[k] = part_sum(k, core)
        if n == 0:
            beside(order[-1]).start()
    for n, k in enumerate(order):
        beside(k).wait_recv()
        both = rown_ref[k] + rrecv_ref[k].astype(F32)
        if n > 0:
            along(order[n - 1]).start()
        if k > 0:
            rsend_ref[chips + k] = both.astype(BF)
    result = both
    for u in range(1, GROUP):
        grad_copy(u).wait_send()
    for k in range(chips):
        beside(k).wait_send()
    for k in (1, 3, 2):
        along(k).wait_recv()
        result = result + rrecv_ref[chips + k].astype(F32)
    out_ref[...] = result
    for k in range(1, chips):
        along(k).wait_send()


def vspec():
    return pl.BlockSpec(memory_space=pltpu.VMEM)


def body(
    emb_table, versions, conf_local, conf_version, conf_values, owners, row_local, lengths,
    dense_out, labels, cross_down, cross_up, cross_bias, head_weight,
):
    rows_dev, emb_width = emb_table.shape
    samples, features, slot_count = row_local.shape
    width, shard = cross_down.shape[1:]
    rank = shard * COPIES
    bags = samples * features
    total = PEERS * SLOTS
    DMA = pltpu.SemaphoreType.DMA
    hbm = pl.BlockSpec(memory_space=pl.ANY)
    logits, emb_grad = pl.pallas_call(
        step_kernel,
        out_shape=(
            jax.ShapeDtypeStruct((samples,), F32),
            jax.ShapeDtypeStruct((rows_dev // COPIES, emb_width), F32),
        ),
        in_specs=[hbm] * 14,
        out_specs=(vspec(), vspec()),
        scratch_shapes=[
            VM((features, 1, samples), jnp.int32),
            VM((features, slot_count, samples), jnp.int32),
            VM((features, samples), jnp.int32),
            VM((1, rows_dev), jnp.int32),
            VM((1, conf_local.shape[0]), jnp.int32),
            VM((1, conf_local.shape[0]), jnp.int32),
            VM(dense_out.shape, BF),
            VM((1, samples), jnp.int32),
            VM((1, width), F32),
            VM((width // LANES, LANES), F32),
            VM((features, samples), jnp.int32),
            VM((1, width), F32),
            VM((rows_dev, LANES), F32),
            VM((conf_local.shape[0], LANES), F32),
            VM((features * PEERS, samples), BF),
            VM((features * PEERS, 2 * samples), F32),
            VM((PEERS, bags), BF),
            VM((PARTS * SLOTS, bags), BF),
            VM((PEERS, 2, LANES), jnp.int32),
            VM((PEERS, 2, LANES), jnp.int32),
            VM((features, samples), jnp.int32),
            VM((PEERS, LANES), jnp.int32),
            pltpu.SMEM((features, samples), jnp.int32),
            pltpu.SMEM((PEERS, LANES), jnp.int32),
            VM((rows_dev, 2 * LANES), BF),
            VM((ASK * SLOTS, rows_dev), BF),
            VM((total, LANES), BF),
            VM((total, LANES), BF),
            VM((total, LANES), F32),
            VM((samples // 8, 8, width), F32),
            VM((samples, width), F32),
            VM((bags, LANES), F32),
            VM((rank, width), BF),
            VM((rank, width), BF),
            VM((SLOTS, LANES), F32),
            VM((PEERS, SLOTS, LANES), BF),
            VM((PEERS, LANES, LANES), BF),
            VM((rows_dev, GROUP * LANES), BF),
            VM((rows_dev, LANES), F32),
            VM((COPIES // 2, rows_dev // COPIES, LANES), F32),
            VM((COPIES, rows_dev // COPIES, LANES), BF),
            VM((COPIES, rows_dev // COPIES, LANES), BF),
            DMA((PEERS,)), DMA((PEERS,)), DMA((PEERS,)), DMA((PEERS,)), DMA((PEERS,)), DMA((PEERS,)),
            DMA((2, 4)), DMA((2, 4)), DMA((2, 4)), DMA((2, 4)),
            DMA((COPIES,)), DMA((COPIES,)),
            DMA((19,)),
        ],
        compiler_params=pltpu.CompilerParams(
            collective_id=0, has_side_effects=True, vmem_limit_bytes=60 * 1024 * 1024
        ),
        name="step",
    )(
        jnp.transpose(owners, (1, 2, 0)),
        jnp.transpose(row_local, (1, 2, 0)),
        lengths.T,
        versions.reshape(1, -1),
        conf_local.reshape(1, -1),
        conf_version.reshape(1, -1),
        emb_table,
        conf_values,
        dense_out,
        labels.reshape(1, -1),
        cross_down[0].T,
        cross_up[0],
        cross_bias,
        head_weight.reshape(-1, LANES),
    )
    return (logits, emb_grad)


def solution(mesh):
    in_specs = (
        P("table", None),
        P("table"),
        P("table"),
        P("table"),
        P("table", None),
        P(("table", "dp"), None, None),
        P(("table", "dp"), None, None),
        P(("table", "dp"), None),
        P(("table", "dp"), None),
        P(("table", "dp")),
        P(None, None, "dp"),
        P(None, "dp", None),
        P(),
        P(),
    )
    out_specs = (P(("table", "dp")), P(("table", "dp"), None))
    return jax.shard_map(body, mesh=mesh, in_specs=in_specs, out_specs=out_specs, check_vma=False)
```

```python
import jax
import jax.numpy as jnp
from jax import lax
from jax.experimental import pallas as pl
from jax.experimental.pallas import tpu as pltpu
from jax.sharding import PartitionSpec as P

loss_scale = 64.0
PEERS = 64
COPIES = 8
RING_Y = 4
RING_Z = 16
SLOTS = 80
SENT = 78
ASK = 2
LANES = 128
GROUP = 8
DEAD = 2048
PARTS = 7
VM = pltpu.VMEM
MESH = pl.DeviceIdType.MESH
NT = (((1,), (1,)), ((), ()))
BF = jnp.bfloat16
F32 = jnp.float32


def offset_of(j):
    t = j % RING_Z
    half = (t + 1) // 2
    odd = t % 2
    return j // RING_Z, odd * half + (1 - odd) * (RING_Z - half)


def shifted(j, here, sign):
    dy, dz = offset_of(j)
    y = (here // RING_Z + RING_Y + sign * dy) % RING_Y
    z = (here % RING_Z + 2 * RING_Z + sign * dz) % RING_Z
    return y * RING_Z + z


def slot_of_owner(own, here):
    dy = (own // RING_Z - here // RING_Z + RING_Y) & (RING_Y - 1)
    dz = (own % RING_Z - here % RING_Z + RING_Z) & (RING_Z - 1)
    t = jnp.where(dz == 0, 0, jnp.where(dz <= RING_Z // 2, 2 * dz - 1, 2 * (RING_Z - dz)))
    return dy * RING_Z + t


def step_kernel(
    own_hbm, row_hbm, len_hbm, ver_hbm, loc_hbm, cver_hbm, table_hbm, conf_hbm,
    dense_hbm, label_hbm, downl_ref, upl_ref, bias_hbm, heads_hbm,
    logit_ref, out_ref,
    own_ref, row_ref, len_ref, ver_ref, loc_ref, cver_ref, dense_ref, label_ref, bias_ref, heads_ref,
    own_s, head_ref, table_ref, conf_ref, hits_ref, prior_ref, wide_ref, placed_ref, req_ref, asked_ref, pos_v, inv_v, pos_s, inv_s,
    tab_ref, hot_ref, found_ref, ans_ref, rows_ref, base_ref, factor_ref, back_ref,
    down_ref, up_ref, stage_ref, gsend_ref, grecv_ref, hot2_ref, acc_ref, rown_ref, rsend_ref, rrecv_ref,
    q_send, q_recv, a_send, a_recv, g_send, g_recv, w_send, w_recv, c_send, c_recv, r_send, r_recv,
    l_sem,
):
    table_at = lax.axis_index("table")
    dp_at = lax.axis_index("dp")
    features, samples = len_hbm.shape
    total = PEERS * SLOTS
    width = bias_ref.shape[1]
    shard = downl_ref.shape[0]
    blocks = table_ref.shape[0] // LANES

    barrier = pltpu.get_barrier_semaphore()

    def greet(i, carry):
        pl.semaphore_signal(
            barrier, inc=1, device_id=(shifted(PEERS - i, table_at, 1), dp_at), device_id_type=MESH
        )
        return carry

    lax.fori_loop(1, PEERS, greet, 0)
    core, chip = dp_at % 2, dp_at // 2
    chips = COPIES // 2
    for k in range(1, chips):
        pl.semaphore_signal(
            barrier, inc=1, device_id=(table_at, ((chip + k) % chips) * 2 + core),
            device_id_type=MESH,
        )
    pl.semaphore_signal(
        barrier, inc=1, device_id=(table_at, chip * 2 + 1 - core), device_id_type=MESH
    )
    sources = (
        (own_hbm, own_ref), (row_hbm, row_ref), (len_hbm, len_ref), (ver_hbm, ver_ref),
        (loc_hbm, loc_ref), (cver_hbm, cver_ref), (dense_hbm, dense_ref), (label_hbm, label_ref),
        (bias_hbm, bias_ref), (heads_hbm, heads_ref), (table_hbm, table_ref), (conf_hbm, conf_ref),
    )
    loads = [
        pltpu.make_async_copy(src, dst, l_sem.at[7 + n]) for n, (src, dst) in enumerate(sources)
    ]
    for load in loads:
        load.start()
    grecv_ref[:, SENT:LANES, :] = jnp.zeros((PEERS, LANES - SENT, LANES), BF)
    for load in loads[:3]:
        load.wait()
    own_s[...] = slot_of_owner(own_ref[:, 0, :], table_at)

    holder = lax.broadcasted_iota(jnp.int32, (PEERS, samples), 0)

    def mark_hits(f, carry):
        hit = jnp.where(own_s[pl.ds(f, 1), :] == holder, 1.0, 0.0).astype(BF)
        hits_ref[pl.ds(pl.multiple_of(f * PEERS, PEERS), PEERS), :] = hit
        wide_ref[:, pl.ds(pl.multiple_of(f * LANES, LANES), LANES)] = hit
        return carry

    lax.fori_loop(0, features, mark_hits, 0, unroll=13)
    row_at = lax.broadcasted_iota(jnp.int32, (samples, 2 * samples), 0)
    col_at = lax.broadcasted_iota(jnp.int32, (samples, 2 * samples), 1)
    before = jnp.where((row_at < col_at) | (col_at >= samples), 1.0, 0.0).astype(BF)
    prior_ref[...] = jnp.dot(hits_ref[...], before, preferred_element_type=F32)
    slot = lax.broadcasted_iota(jnp.int32, (SLOTS, samples), 0).astype(F32)
    sample = lax.broadcasted_iota(jnp.int32, (1, samples), 1).astype(F32)

    def rank_bags(f, carry):
        at = pl.ds(pl.multiple_of(f * PEERS, PEERS), PEERS)
        onehot = hits_ref[at, :].astype(F32)
        rank = jnp.sum(onehot * (prior_ref[at, 0:samples] + carry), axis=0, keepdims=True)
        owner = own_s[pl.ds(f, 1), :]
        pos_v[pl.ds(f, 1), :] = owner * SLOTS + jnp.clip(rank.astype(jnp.int32), 0, SLOTS - 1)
        both = row_ref[f]
        first = both[0:1, :]
        second = jnp.where(len_ref[pl.ds(f, 1), :] > 1, both[1:2, :], DEAD)
        here = slot == rank
        lanes = pl.ds(pl.multiple_of(f * LANES, LANES), LANES)
        values = []
        for value in (first, second):
            values.append((value >> 7).astype(F32))
            values.append((value & 127).astype(F32))
        values.append(jnp.full((1, samples), f, jnp.int32).astype(F32))
        values.append(sample)
        values.append(jnp.ones((1, samples), F32))
        for p, value in enumerate(values):
            placed = jnp.where(here, value, 0.0).astype(BF)
            placed_ref[p * SLOTS : (p + 1) * SLOTS, lanes] = placed
        return carry + prior_ref[at, samples : 2 * samples]

    lax.fori_loop(0, features, rank_bags, jnp.zeros((PEERS, samples), F32), unroll=13)
    packed = lax.dot_general(wide_ref[...], placed_ref[...], NT, preferred_element_type=F32)
    part = [packed[:, p * SLOTS : (p + 1) * SLOTS] for p in range(PARTS)]
    filled = part[6] > 0.5
    dead_tail = jnp.full((PEERS, LANES - SLOTS), DEAD, jnp.int32)
    for q in range(2):
        ids = (part[2 * q] * 128.0 + part[2 * q + 1]).astype(jnp.int32)
        ids = jnp.where(filled, ids, DEAD)
        req_ref[:, q, :] = jnp.concatenate([ids, dead_tail], axis=1)
    inverse = (part[4] * 128.0 + part[5]).astype(jnp.int32)
    inverse = jnp.clip(inverse, 0, features * samples - 1)
    inv_v[...] = jnp.concatenate([inverse, jnp.zeros_like(dead_tail)], axis=1)

    to_smem = [
        pltpu.make_async_copy(pos_v, pos_s, l_sem.at[0]),
        pltpu.make_async_copy(inv_v, inv_s, l_sem.at[1]),
    ]
    for copy in to_smem:
        copy.start()
    own_request = pltpu.make_async_copy(req_ref.at[0], asked_ref.at[0], l_sem.at[2])
    own_request.start()

    pl.semaphore_wait(barrier, PEERS - 1 + chips)

    def request_copy(j):
        return pltpu.make_async_remote_copy(
            src_ref=req_ref.at[j], dst_ref=asked_ref.at[j],
            send_sem=q_send.at[j], recv_sem=q_recv.at[j],
            device_id=(shifted(j, table_at, 1), dp_at), device_id_type=MESH,
        )

    def send_request(i, carry):
        request_copy(PEERS - i).start()
        return carry

    lax.fori_loop(1, PEERS, send_request, 0)

    weights = ((downl_ref, down_ref), (upl_ref, up_ref))

    def shard_rows(d):
        return pl.ds(pl.multiple_of(d * shard, shard), shard)

    def across(w, k):
        local, full = weights[w]
        return pltpu.make_async_remote_copy(
            src_ref=local, dst_ref=full.at[shard_rows(dp_at)],
            send_sem=w_send.at[w, k], recv_sem=w_recv.at[w, k],
            device_id=(table_at, ((chip + k) % chips) * 2 + core), device_id_type=MESH,
        )

    def pass_on(w, k):
        local, full = weights[w]
        rows = shard_rows(((chip - k + chips) % chips) * 2 + core)
        return pltpu.make_async_remote_copy(
            src_ref=local if k == 0 else full.at[rows], dst_ref=full.at[rows],
            send_sem=c_send.at[w, k], recv_sem=c_recv.at[w, k],
            device_id=(table_at, chip * 2 + 1 - core), device_id_type=MESH,
        )

    own_weights = []
    for w in range(2):
        for k in (1, 3, 2):
            across(w, k).start()
        pass_on(w, 0).start()
        copy = pltpu.make_async_copy(
            weights[w][0], weights[w][1].at[shard_rows(dp_at)], l_sem.at[3 + w]
        )
        copy.start()
        own_weights.append(copy)

    for load in loads[3:]:
        load.wait()
    confs = conf_ref.shape[0]
    versions = ver_ref[...]
    pair = jnp.concatenate(
        [(versions >> 7).astype(F32), (versions & 127).astype(F32)]
        + [jnp.zeros((6, versions.shape[1]), F32)], axis=0,
    ).astype(BF)
    local = loc_ref[...]
    line = lax.broadcasted_iota(jnp.int32, (LANES, confs), 0)

    def seen(k, carry):
        hit = jnp.where(line + k * LANES == local, 1.0, 0.0).astype(BF)
        hot2_ref[pl.ds(pl.multiple_of(k * LANES, LANES), LANES), 0:confs] = hit
        return carry

    lax.fori_loop(0, blocks, seen, 0)
    current = jnp.dot(pair, hot2_ref[:, 0:confs], preferred_element_type=F32)
    current = current[0:1, :] * 128.0 + current[1:2, :]
    newer = jnp.where(cver_ref[...].astype(F32) > current, 1.0, 0.0)
    conf = conf_ref[...]
    conf_high = conf.astype(BF)
    conf_low = (conf - conf_high.astype(F32)).astype(BF)
    fresh = jnp.concatenate([conf_high, conf_low, jnp.ones((confs, LANES), BF)], axis=1)

    def renew(k, carry):
        at = pl.ds(pl.multiple_of(k * LANES, LANES), LANES)
        mask = (hot2_ref[at, 0:confs].astype(F32) * newer).astype(BF)
        got = jnp.dot(mask, fresh, preferred_element_type=F32)
        now = table_ref[at, :]
        high = now.astype(BF).astype(F32)
        take = got[:, 2 * LANES : 3 * LANES] > 0.5
        tab_ref[at, 0:LANES] = jnp.where(take, got[:, 0:LANES], high).astype(BF)
        low = jnp.where(take, got[:, LANES : 2 * LANES], now - high)
        tab_ref[at, LANES : 2 * LANES] = low.astype(BF)
        return carry

    lax.fori_loop(0, blocks, renew, 0)

    own_request.wait()
    lane = lax.broadcasted_iota(jnp.int32, (SLOTS, LANES), 1)
    zero = jnp.zeros((SLOTS, LANES), BF)

    def chunk(ref, j):
        return ref.at[pl.ds(pl.multiple_of(j * SLOTS, SLOTS), SENT)]

    def group_at(i):
        late = (i + 3) // 8
        return (1 - late) * (2 * i - 1) + late * (16 - 2 * i) + (8 - i) // 8

    def answer_copy(j):
        return pltpu.make_async_remote_copy(
            src_ref=chunk(found_ref, j), dst_ref=chunk(ans_ref, j),
            send_sem=a_send.at[j], recv_sem=a_recv.at[j],
            device_id=(shifted(j, table_at, -1), dp_at), device_id_type=MESH,
        )

    own_answer = pltpu.make_async_copy(
        found_ref.at[0:SENT], ans_ref.at[0:SENT], l_sem.at[5]
    )

    def first_slot(i):
        per = GROUP // ASK
        return group_at(i // per) * GROUP + (i % per) * ASK

    def send_answers(i):
        start = first_slot(i)

        @pl.when(i > 0)
        def _():
            answer_copy(start).start()

        for u in range(1, ASK):
            answer_copy(start + u).start()

    def answer_group(i, carry):
        start = first_slot(i)

        @pl.when(i > 0)
        def _():
            request_copy(start).wait_recv()

        for u in range(1, ASK):
            request_copy(start + u).wait_recv()
        columns = jnp.transpose(
            jnp.concatenate([asked_ref[start + u] for u in range(ASK)], axis=0)
        )
        for u in range(ASK):
            low, high = [], []
            for q in range(2):
                at = 2 * u + q
                ids = jnp.broadcast_to(columns[0:SLOTS, at : at + 1], (SLOTS, LANES))
                low.append(jnp.where((ids & 127) == lane, 1.0, 0.0).astype(BF))
                high.append((ids >> 7).astype(F32).astype(BF))
            for k in range(blocks):
                k16 = BF(k)
                hot = jnp.where(high[0] == k16, low[0], zero) + jnp.where(
                    high[1] == k16, low[1], zero
                )
                hot_ref[u * SLOTS : (u + 1) * SLOTS, k * LANES : (k + 1) * LANES] = hot
        both = jnp.dot(hot_ref[...], tab_ref[...], preferred_element_type=F32)
        found_ref[pl.ds(pl.multiple_of(start * SLOTS, SLOTS), ASK * SLOTS), :] = (
            both[:, :LANES] + both[:, LANES:]
        ).astype(BF)

        @pl.when(i > 0)
        def _():
            send_answers(i - 1)

        return carry

    lax.fori_loop(0, PEERS // ASK, answer_group, 0)
    own_answer.start()
    send_answers(jnp.int32(PEERS // ASK - 1))

    acc_ref[...] = jnp.zeros_like(acc_ref)
    for f in range(features + 1):
        head_ref[:, f * LANES : (f + 1) * LANES] = heads_ref[f : f + 1, :]
    base_ref[:, :, 0:LANES] = dense_ref[...].astype(F32).reshape(samples // 8, 8, LANES)
    labels = jnp.broadcast_to(label_ref[...], (samples, samples)).astype(F32)
    labels = jnp.transpose(labels)[:, 0:1]
    for k in (1, 3, 2):
        for w in range(2):
            across(w, k).wait_recv()
            pass_on(w, k).start()
    own_answer.wait()
    rows_ref[0:SLOTS, :] = ans_ref[0:SLOTS, :].astype(F32)

    def take_answer(j, carry):
        answer_copy(j).wait_recv()
        at = pl.ds(pl.multiple_of(j * SLOTS, SLOTS), SLOTS)
        rows_ref[at, :] = ans_ref[at, :].astype(F32)
        return carry

    lax.fori_loop(1, PEERS, take_answer, 0)
    for copy in to_smem:
        copy.wait()

    def fetch(block, carry):
        b0 = block * 8
        for f in range(features):
            for u in range(8):
                row = rows_ref[pl.ds(pos_s[f, b0 + u], 1), :]
                base_ref[block, u : u + 1, (f + 1) * LANES : (f + 2) * LANES] = row
        return carry

    lax.fori_loop(0, samples // 8, fetch, 0)
    for w in range(2):
        own_weights[w].wait()
        for k in (0, 1, 3, 2):
            pass_on(w, k).wait_recv()
    inputs = base_ref[...].reshape(samples, width).astype(BF)
    crossed = lax.dot_general(inputs, down_ref[...], NT, preferred_element_type=F32).astype(BF)
    base = inputs.astype(F32)
    head = head_ref[...]
    factor = jnp.dot(crossed, up_ref[...], preferred_element_type=F32) + bias_ref[...]
    factor_ref[...] = factor
    logits = jnp.sum((base * factor + base) * head, axis=1, keepdims=True)
    logit_ref[...] = jnp.transpose(jnp.broadcast_to(logits, (samples, samples)))[0, :]
    signal = loss_scale * (jax.nn.sigmoid(logits) - labels)
    state = signal * head
    lift = (state * base).astype(BF)
    cross = lax.dot_general(lift, up_ref[...], NT, preferred_element_type=F32).astype(BF)
    back = state + jnp.dot(cross, down_ref[...], preferred_element_type=F32) + state * factor_ref[...]
    for f in range(features):
        back_ref[f * samples : (f + 1) * samples, :] = back[:, (f + 1) * LANES : (f + 2) * LANES]

    def grad_copy(j):
        return pltpu.make_async_remote_copy(
            src_ref=gsend_ref.at[j, pl.ds(0, SENT)], dst_ref=grecv_ref.at[j, pl.ds(0, SENT)],
            send_sem=g_send.at[j], recv_sem=g_recv.at[j],
            device_id=(shifted(j, table_at, 1), dp_at), device_id_type=MESH,
        )

    def place(i, carry):
        j = PEERS - 1 - i
        for r in range(SLOTS):
            stage_ref[r : r + 1, :] = back_ref[pl.ds(inv_s[j, r], 1), :]
        gsend_ref[j] = stage_ref[...].astype(BF)

        @pl.when(i > 0)
        def _():
            grad_copy(j + 1).start()

        return carry

    lax.fori_loop(0, PEERS, place, 0)
    own_grad = pltpu.make_async_copy(
        gsend_ref.at[0, pl.ds(0, SENT)], grecv_ref.at[0, pl.ds(0, SENT)], l_sem.at[6]
    )
    own_grad.start()

    def drain(j, carry):
        request_copy(j).wait_send()
        answer_copy(j).wait_send()
        return carry

    lax.fori_loop(1, PEERS, drain, 0)
    for w in range(2):
        for k in range(1, chips):
            across(w, k).wait_send()
        for k in range(chips):
            pass_on(w, k).wait_send()

    spot = lax.broadcasted_iota(jnp.int32, (LANES, LANES), 0)
    nothing = jnp.zeros((LANES, LANES), BF)

    def hot_rows(j, u):
        both = asked_ref[j]
        low, high = [], []
        for q in range(2):
            ids = both[q : q + 1, :]
            low.append(jnp.where((ids & 127) == spot, 1.0, 0.0).astype(BF))
            wide = jnp.broadcast_to((ids >> 7).astype(F32), (LANES, LANES))
            high.append(wide.astype(BF))
        for k in range(blocks):
            k16 = BF(k)
            hot = jnp.where(high[0] == k16, low[0], nothing) + jnp.where(
                high[1] == k16, low[1], nothing
            )
            hot2_ref[k * LANES : (k + 1) * LANES, u * LANES : (u + 1) * LANES] = hot

    def grads_of(g):
        for u in range(GROUP):
            hot_rows(g * GROUP + u, u)
        for u in range(GROUP - 1, 0, -1):
            grad_copy(g * GROUP + u).wait_recv()

    def group_rows(g):
        grads = grecv_ref[pl.ds(pl.multiple_of(g * GROUP, GROUP), GROUP)]
        return grads.reshape(GROUP * LANES, LANES)

    def take_group(i, carry):
        g = PEERS // GROUP - 1 - i
        grads_of(g)
        grad_copy(g * GROUP).wait_recv()
        acc_ref[...] += jnp.dot(hot2_ref[...], group_rows(g), preferred_element_type=F32)
        for u in range(GROUP):
            grad_copy(g * GROUP + u).wait_send()
        return carry

    lax.fori_loop(0, PEERS // GROUP - 1, take_group, 0)
    grads_of(0)
    own_grad.wait()

    part_rows = out_ref.shape[0]
    last = grecv_ref[0:GROUP].reshape(GROUP * LANES, LANES)

    def part_at(k, side):
        target = ((chip + k) % chips) * 2 + side
        return pl.ds(pl.multiple_of(target * part_rows, part_rows), part_rows)

    def part_sum(k, side):
        at = part_at(k, side)
        return acc_ref[at, :] + jnp.dot(hot2_ref[at, :], last, preferred_element_type=F32)

    def beside(k):
        return pltpu.make_async_remote_copy(
            src_ref=rsend_ref.at[k], dst_ref=rrecv_ref.at[k],
            send_sem=r_send.at[k], recv_sem=r_recv.at[k],
            device_id=(table_at, chip * 2 + 1 - core), device_id_type=MESH,
        )

    def along(k):
        return pltpu.make_async_remote_copy(
            src_ref=rsend_ref.at[chips + k], dst_ref=rrecv_ref.at[chips + k],
            send_sem=r_send.at[chips + k], recv_sem=r_recv.at[chips + k],
            device_id=(table_at, ((chip + k) % chips) * 2 + core), device_id_type=MESH,
        )

    order = (2, 3, 1, 0)
    for n, k in enumerate(order):
        rsend_ref[k] = part_sum(k, 1 - core).astype(BF)
        if n > 0:
            beside(order[n - 1]).start()
    for n, k in enumerate(order):
        rown_ref[k] = part_sum(k, core)
        if n == 0:
            beside(order[-1]).start()
    for n, k in enumerate(order):
        beside(k).wait_recv()
        both = rown_ref[k] + rrecv_ref[k].astype(F32)
        if n > 0:
            along(order[n - 1]).start()
        if k > 0:
            rsend_ref[chips + k] = both.astype(BF)
    result = both
    for u in range(1, GROUP):
        grad_copy(u).wait_send()
    for k in range(chips):
        beside(k).wait_send()
    for k in (1, 3, 2):
        along(k).wait_recv()
        result = result + rrecv_ref[chips + k].astype(F32)
    out_ref[...] = result
    for k in range(1, chips):
        along(k).wait_send()


def vspec():
    return pl.BlockSpec(memory_space=pltpu.VMEM)


def body(
    emb_table, versions, conf_local, conf_version, conf_values, owners, row_local, lengths,
    dense_out, labels, cross_down, cross_up, cross_bias, head_weight,
):
    rows_dev, emb_width = emb_table.shape
    samples, features, slot_count = row_local.shape
    width, shard = cross_down.shape[1:]
    rank = shard * COPIES
    bags = samples * features
    total = PEERS * SLOTS
    DMA = pltpu.SemaphoreType.DMA
    hbm = pl.BlockSpec(memory_space=pl.ANY)
    logits, emb_grad = pl.pallas_call(
        step_kernel,
        out_shape=(
            jax.ShapeDtypeStruct((samples,), F32),
            jax.ShapeDtypeStruct((rows_dev // COPIES, emb_width), F32),
        ),
        in_specs=[hbm] * 14,
        out_specs=(vspec(), vspec()),
        scratch_shapes=[
            VM((features, 1, samples), jnp.int32),
            VM((features, slot_count, samples), jnp.int32),
            VM((features, samples), jnp.int32),
            VM((1, rows_dev), jnp.int32),
            VM((1, conf_local.shape[0]), jnp.int32),
            VM((1, conf_local.shape[0]), jnp.int32),
            VM(dense_out.shape, BF),
            VM((1, samples), jnp.int32),
            VM((1, width), F32),
            VM((width // LANES, LANES), F32),
            VM((features, samples), jnp.int32),
            VM((1, width), F32),
            VM((rows_dev, LANES), F32),
            VM((conf_local.shape[0], LANES), F32),
            VM((features * PEERS, samples), BF),
            VM((features * PEERS, 2 * samples), F32),
            VM((PEERS, bags), BF),
            VM((PARTS * SLOTS, bags), BF),
            VM((PEERS, 2, LANES), jnp.int32),
            VM((PEERS, 2, LANES), jnp.int32),
            VM((features, samples), jnp.int32),
            VM((PEERS, LANES), jnp.int32),
            pltpu.SMEM((features, samples), jnp.int32),
            pltpu.SMEM((PEERS, LANES), jnp.int32),
            VM((rows_dev, 2 * LANES), BF),
            VM((ASK * SLOTS, rows_dev), BF),
            VM((total, LANES), BF),
            VM((total, LANES), BF),
            VM((total, LANES), F32),
            VM((samples // 8, 8, width), F32),
            VM((samples, width), F32),
            VM((bags, LANES), F32),
            VM((rank, width), BF),
            VM((rank, width), BF),
            VM((SLOTS, LANES), F32),
            VM((PEERS, SLOTS, LANES), BF),
            VM((PEERS, LANES, LANES), BF),
            VM((rows_dev, GROUP * LANES), BF),
            VM((rows_dev, LANES), F32),
            VM((COPIES // 2, rows_dev // COPIES, LANES), F32),
            VM((COPIES, rows_dev // COPIES, LANES), BF),
            VM((COPIES, rows_dev // COPIES, LANES), BF),
            DMA((PEERS,)), DMA((PEERS,)), DMA((PEERS,)), DMA((PEERS,)), DMA((PEERS,)), DMA((PEERS,)),
            DMA((2, 4)), DMA((2, 4)), DMA((2, 4)), DMA((2, 4)),
            DMA((COPIES,)), DMA((COPIES,)),
            DMA((19,)),
        ],
        compiler_params=pltpu.CompilerParams(
            collective_id=0, has_side_effects=True, vmem_limit_bytes=50 << 20
        ),
        name="step",
    )(
        jnp.transpose(owners, (1, 2, 0)),
        jnp.transpose(row_local, (1, 2, 0)),
        lengths.T,
        versions.reshape(1, -1),
        conf_local.reshape(1, -1),
        conf_version.reshape(1, -1),
        emb_table,
        conf_values,
        dense_out,
        labels.reshape(1, -1),
        cross_down[0].T,
        cross_up[0],
        cross_bias,
        head_weight.reshape(-1, LANES),
    )
    return (logits, emb_grad)


def solution(mesh):
    in_specs = (
        P("table", None),
        P("table"),
        P("table"),
        P("table"),
        P("table", None),
        P(("table", "dp"), None, None),
        P(("table", "dp"), None, None),
        P(("table", "dp"), None),
        P(("table", "dp"), None),
        P(("table", "dp")),
        P(None, None, "dp"),
        P(None, "dp", None),
        P(),
        P(),
    )
    out_specs = (P(("table", "dp")), P(("table", "dp"), None))
    return jax.shard_map(body, mesh=mesh, in_specs=in_specs, out_specs=out_specs, check_vma=False)
```
